32 devices in a mesh: col: 8 (over z, y), row: 4 (over x, core).
Axes of the slice: x: 2, y: 2, z: 4, core: 2. Of those that a mesh axis runs over, the one named last changes fastest.
Arguments:
- panel: float32 [2, 12288, 6144], P(None, 'row', 'col'), may hold values from -0.078125 to 0.078125
- prior: float32 [6144, 64], P('col'), may hold values from -6 to 6
- right_side: float32 [2, 12288, 64], P(None, 'row'), may hold values from -6 to 6
- coupling: float32 [12288, 12288], P('row', 'col'), may hold values from -0.0546875 to 0.0546875
- inverses: float32 [2, 12288, 12288], P(None, 'row', 'col'), as said below
Outputs:
- solved: float32 [2, 12288, 64], P(None, 'row')
The draws below stay inside these ranges and needn't reach their ends.
Inputs may be any that keep to these rules, and one draw needn't show every extreme that they name: `inverses`: each of the two blocks is zero above its diagonal, and its diagonal lies between 0.5 and 2.
All inputs are finite; a program needn't handle non-finite values.
Results may differ from the reference program's by a relative error of at most 0.00011.
Values sent between devices are 32-bit elements; how exact they have to be, the bound alone decides.
A program may use at most 128 MiB of HBM per device.

```python
import math
import jax
import jax.numpy as jnp
from jax import lax

NB = 12288
R = 64
K = 6144


def draw_inverses(key, part):
    inner = jax.random.fold_in(key, 11)
    key_below, key_diag = jax.random.split(inner)
    rows = lax.broadcasted_iota(jnp.int32, (2, NB, NB), 1)
    cols = lax.broadcasted_iota(jnp.int32, (2, NB, NB), 2)
    below = jax.random.normal(key_below, (2, NB, NB), jnp.float32) / math.sqrt(NB)
    diag = jnp.exp(jax.random.uniform(key_diag, (2, NB, 1), jnp.float32, math.log(0.5), math.log(2.0)))
    return jnp.where(rows > cols, below, jnp.where(rows == cols, diag, 0.0))


def levels(rng, extent, cuts, low, high):
    level = 1.0
    for axis_at, blocks in cuts:
        steps = jax.random.uniform(jax.random.fold_in(jax.random.fold_in(rng, 6), axis_at), (blocks,), jnp.float32, low / len(cuts), high / len(cuts))
        level = level * jnp.repeat(jnp.exp(steps), extent[axis_at] // blocks).reshape((-1,) + (1,) * (len(extent) - 1 - axis_at))
    return level


def normal_values(own_key, dims, spread, limit, pieces=(), kind=jnp.bfloat16):
    values = spread * jax.random.normal(own_key, dims, jnp.float32)
    if pieces:
        values = values * levels(own_key, dims, pieces, -0.22, 0.18)
    return jnp.clip(values, -limit, limit).astype(kind)


def setup_inputs(seed: int = 0) -> dict:
    key_list = jax.random.split(jax.random.key(seed), 6)
    return {
        "panel": normal_values(key_list[0], (2, NB, K), K ** -0.5, 0.078125, ((1, 4), (2, 8)), jnp.float32),
        "prior": normal_values(key_list[1], (K, R), 1.0, 6.0, ((0, 8),), jnp.float32),
        "right_side": normal_values(key_list[2], (2, NB, R), 1.0, 6.0, ((1, 4),), jnp.float32),
        "coupling": normal_values(key_list[3], (NB, NB), NB ** -0.5, 0.0546875, ((0, 4), (1, 8)), jnp.float32),
        "inverses": draw_inverses(jax.random.fold_in(key_list[5], 71), 0),
    }


def reference(panel, prior, right_side, coupling, inverses):
    highest = lax.Precision.HIGHEST
    carried = jnp.einsum("bik,kr->bir", panel, prior, precision=highest)
    first = right_side[0] - carried[0]
    leading = jnp.dot(inverses[0], first, precision=highest)
    second = right_side[1] - (carried[1] + jnp.dot(coupling, leading, precision=highest))
    trailing = jnp.dot(inverses[1], second, precision=highest)
    return jnp.stack([leading, trailing])
```

```python
import functools
import jax
import jax.numpy as jnp
from jax import lax
from jax.experimental import pallas as pl
from jax.experimental.pallas import tpu as pltpu
from jax.sharding import PartitionSpec as P

F32, BF16 = jnp.float32, jnp.bfloat16
SUBS = 2
NT = (((1,), (1,)), ((), ()))


def kernel(q, nr, panel, prior, rs, coup, inv, out, part, part1, ra, rb, tv, xv, wv, w0, pbuf, buf0, buf1, rsv,
           psem, sem0, sem1, rsem, a_s, a_r, b_s, b_r, c1_s, x_r, c2_s, d_s, d_r, dy_s, dy_r):
    zn = nr
    nx = nr // 2
    r, pr = part.shape[2:]
    subs = range(SUBS)
    sub = [pl.ds(h * (r // SUBS), r // SUBS) for h in subs]
    col = lax.axis_index("col")
    i = lax.axis_index("row")
    z, y = lax.div(col, q), lax.rem(col, q)
    below = z <= i
    hub = z == i
    direct = lax.rem(i, 2) == lax.rem(z, 2)
    far = jnp.logical_and(direct, jnp.logical_not(hub))
    sibling = i + 1 - 2 * lax.rem(i, 2)

    def dev(zz, yy, ii):
        return {"col": zz * q + yy, "row": ii}

    def zfwd(k):
        return lax.rem(z + 1 + k, zn)

    def zback(k):
        return lax.rem(z + zn - 1 - k, zn)

    def yfwd(m):
        return lax.rem(y + 1 + m, q)

    def yback(m):
        return lax.rem(y + q - 1 - m, q)

    def remote(src, dst, ss, rr, to):
        return pltpu.make_async_remote_copy(
            src_ref=src, dst_ref=dst, send_sem=ss, recv_sem=rr, device_id=to, device_id_type=pl.DeviceIdType.MESH)

    def rows_of(m, k):
        return pl.ds(pl.multiple_of((yfwd(m) * zn + zfwd(k)) * pr, pr), pr)

    def load(src, dst, sem, m, k):
        rows = rows_of(m, k)
        return pltpu.make_async_copy(src.at[rows, :], dst.at[rows, :], sem.at[m * zn + k])

    def load_all(src, dst, sem):
        for m in range(q):
            pl.loop(0, zn)(lambda k, m=m: load(src, dst, sem, m, k).start())

    load_all(panel.at[0], pbuf, psem)

    def piece(ref, b, yy, zz):
        if len(ref.shape) == 4:
            return ref.at[b, yy * zn + zz]
        return ref.at[b, :, pl.ds(pl.multiple_of((yy * zn + zz) * pr, pr), pr)]

    rs_copies = [pltpu.make_async_copy(piece(rs, b, y, z), rsv.at[b], rsem.at[b]) for b in range(2)]
    for c in rs_copies:
        c.start()
    pl.when(below)(lambda: load_all(inv.at[0], buf0, sem0))

    barrier = pltpu.get_barrier_semaphore()
    for k in range(zn - 1):
        pl.semaphore_signal(barrier, inc=1, device_id=dev(zfwd(k), y, i), device_id_type=pl.DeviceIdType.MESH)
    for m in range(q - 1):
        pl.semaphore_signal(barrier, inc=1, device_id=dev(z, yfwd(m), i), device_id_type=pl.DeviceIdType.MESH)
    for n in range(nr - 1):
        pl.semaphore_signal(barrier, inc=1, device_id=dev(z, y, lax.rem(i + 1 + n, nr)), device_id_type=pl.DeviceIdType.MESH)

    @pl.when(far)
    def _():
        for k in range(zn):
            pl.semaphore_signal(barrier, inc=1, device_id=dev(k, y, z), device_id_type=pl.DeviceIdType.MESH)

    def split(x):
        high = x.astype(BF16).astype(F32)
        return jnp.concatenate([high, x - high], axis=0).T.astype(BF16)

    w0[...] = split(prior[...])
    for c in rs_copies:
        c.wait()
    pl.semaphore_wait(barrier, zn - 1 + q - 1 + nr - 1 + nx - 1)

    def product(buf, w, m, k):
        a = buf[rows_of(m, k), :]
        a1 = a.astype(BF16)
        a2 = (a - a1.astype(F32)).astype(BF16)
        p = jnp.dot(jnp.concatenate([a1, a2], axis=0), w[...], preferred_element_type=F32)
        s = (p[:pr] + p[pr:]).T
        return s[:r] + s[r:]

    def a_copy(ph, m, k, h):
        return remote(part.at[yfwd(m), zfwd(k), sub[h]], ra.at[ph, m, k, sub[h]], a_s.at[ph, m, k, h],
                      a_r.at[ph, m, k, h], dev(z, yfwd(m), i))

    def b_copy(ph, k, h):
        return remote(part.at[y, zfwd(k), sub[h]], rb.at[ph, k, sub[h]], b_s.at[ph, k, h], b_r.at[ph, k, h],
                      dev(zfwd(k), y, i))

    def guard(tri, cond, f):
        if tri:
            pl.when(cond)(f)
        else:
            f()

    def reduce(ph, src, buf, sem, w, tri, rhs, emit, add=False, after=None):
        def absorb(k, h):
            val = part[y, zfwd(k), sub[h]]
            for m in range(q - 1):
                a_copy(ph, m, k, h).wait_recv()
                val = val + ra[ph, m, k, sub[h]]
            part[y, zfwd(k), sub[h]] = val
            pl.when(k < zn - 1)(lambda: b_copy(ph, k, h).start())

        def compute():
            for m in range(q):
                @pl.loop(0, zn)
                def _(k):
                    load(src, buf, sem, m, k).wait()
                    val = product(buf, w, m, k)
                    if add:
                        val = val + part1[yfwd(m), zfwd(k)]
                    part[yfwd(m), zfwd(k)] = val
                    if after is not None:
                        load(after, buf, sem, m, k).start()
                    if m < q - 1:
                        a_copy(ph, m, k, 0).start()
                    else:
                        absorb(k, 0)

                if m < q - 1:
                    for h in subs[1:]:
                        pl.loop(0, zn)(lambda k, m=m, h=h: a_copy(ph, m, k, h).start())
            for h in subs[1:]:
                pl.loop(0, zn)(lambda k, h=h: absorb(k, h))

        guard(tri, below, compute)
        if tri:
            @pl.when(jnp.logical_not(below))
            def _():
                part[y, z] = jnp.zeros((r, pr), F32)
        for h in subs:
            for k in range(zn - 1):
                def take(k=k):
                    b_copy(ph, k, h).wait_recv()
                    part[y, z, sub[h]] = part[y, z, sub[h]] + rb[ph, k, sub[h]]

                guard(tri, zback(k) <= i, take)
            val = part[y, z, sub[h]]
            tv[ph, sub[h]] = val if rhs is None else rsv[rhs, sub[h]] - val
            emit(ph, h)

    def drain(ph, tri):
        def waits():
            for h in subs:
                for m in range(q - 1):
                    pl.loop(0, zn)(lambda k, m=m: a_copy(ph, m, k, h).wait_send())
                pl.loop(0, zn - 1)(lambda k: b_copy(ph, k, h).wait_send())

        guard(tri, below, waits)

    def up(ph, n, h):
        return remote(tv.at[ph, sub[h]], xv.at[ph, z, sub[h]], c1_s.at[ph, n, h], x_r.at[ph, z, h],
                      dev(i, y, lax.rem(i + 2 * n, nr)))

    def fwd(ph, s, h):
        there = xv.at[ph, s, sub[h]]
        return remote(there, there, c2_s.at[ph, s, h], x_r.at[ph, s, h], dev(z, y, sibling))

    def rise(ph, h):
        @pl.when(hub)
        def _():
            xv[ph, z, sub[h]] = tv[ph, sub[h]]

        for n in range(1, nx):
            up(ph, n, h).start()
        pl.when(jnp.logical_not(hub))(lambda: up(ph, 0, h).start())

    def spread(ph):
        for h in subs:
            @pl.loop(0, zn)
            def _(k):
                s = lax.rem(z + k, zn)
                pl.when(jnp.logical_not(jnp.logical_and(hub, s == z)))(lambda: fwd(ph, s, h).wait_recv())
                pl.when(direct)(lambda: fwd(ph, s, h).start())
                if h == SUBS - 1:
                    wv[pl.ds(pl.multiple_of(s * pr, pr), pr), :] = split(xv[ph, s])

    def spread_end(ph):
        for h in subs:
            for n in range(1, nx):
                up(ph, n, h).wait_send()
            pl.when(jnp.logical_not(hub))(lambda: up(ph, 0, h).wait_send())
            pl.when(direct)(lambda: pl.loop(0, zn)(lambda s: fwd(ph, s, h).wait_send()))

    def at_out(b, yy, zz, h):
        return piece(out, b, yy, zz).at[sub[h]]

    def dz_copy(b, ph, k, h, zz):
        return remote(tv.at[ph, sub[h]], at_out(b, y, zz, h), d_s.at[b, k, h], d_r.at[b, k, h], dev(zfwd(k), y, i))

    def dy_copy(b, m, slot, s, h, yy):
        return remote(at_out(b, y, s, h), at_out(b, yy, s, h), dy_s.at[b, m, slot, h], dy_r.at[b, m, slot, h],
                      dev(z, yfwd(m), i))

    def publish_z(b, ph, h):
        at_out(b, y, z, h)[...] = tv[ph, sub[h]]
        for k in range(zn - 1):
            dz_copy(b, ph, k, h, z).start()

    def publish_own(b, h):
        for m in range(q - 1):
            dy_copy(b, m, 0, z, h, y).start()

    def publish_y(b, ph, h):
        for k in range(zn - 1):
            dz_copy(b, ph, k, h, zback(k)).wait_recv()
            for m in range(q - 1):
                dy_copy(b, m, k + 1, zback(k), h, y).start()

    def publish_end(b, ph):
        for h in subs:
            for slot in range(zn):
                s = z if slot == 0 else zback(slot - 1)
                for m in range(q - 1):
                    dy_copy(b, m, slot, s, h, yback(m)).wait_recv()
                    dy_copy(b, m, slot, s, h, y).wait_send()
            for k in range(zn - 1):
                dz_copy(b, ph, k, h, z).wait_send()

    def second_carried():
        for m in range(q):
            @pl.loop(0, zn)
            def _(k):
                load(panel.at[1], pbuf, psem, m, k).wait()
                part1[yfwd(m), zfwd(k)] = product(pbuf, w0, m, k)

    def last(ph, h):
        publish_z(1, ph, h)
        publish_own(1, h)

    reduce(0, panel.at[0], pbuf, psem, w0, False, 0, rise, after=panel.at[1])
    second_carried()
    load_all(coup, buf1, sem1)
    spread(0)
    drain(0, False)
    reduce(1, inv.at[0], buf0, sem0, wv, True, None, rise, after=inv.at[1])
    spread(1)
    drain(1, True)
    publish_z(0, 1, 0)
    reduce(2, coup, buf1, sem1, wv, False, 1, rise, add=True)
    publish_own(0, 0)
    publish_y(0, 1, 0)
    spread(2)
    drain(2, False)
    for h in subs[1:]:
        publish_z(0, 1, h)
        publish_own(0, h)
    reduce(3, inv.at[1], buf0, sem0, wv, True, None, last)
    for h in subs[1:]:
        publish_y(0, 1, h)
    for h in subs:
        publish_y(1, 3, h)
    drain(3, True)
    for ph in range(3):
        spread_end(ph)
    publish_end(0, 1)
    publish_end(1, 3)


def paired(panel, prior, rs, coup, inv, out, part, part1, r1, r2, xv, wv, w0, pbuf, buf0, buf1, rsv, priv, lead,
           psem, sem0, sem1, rsem, s1_s, s1_r, s2_s, s2_r, s3_s, s3_r, o_s, o_r, f_s, f_r, l_s, l_r):
    zn = nr = 4
    r, pr = part.shape[2:]
    subs = range(SUBS)
    sub = [pl.ds(n * (r // SUBS), r // SUBS) for n in subs]
    low = [pl.ds(r + n * (r // SUBS), r // SUBS) for n in subs]
    col = lax.axis_index("col")
    i = lax.axis_index("row")
    z, y = lax.div(col, 2), lax.rem(col, 2)
    x, c = lax.div(i, 2), lax.rem(i, 2)
    across = lax.rem(i + 2, nr)
    sibling = i + 1 - 2 * c
    others = [across, lax.rem(sibling + 2, nr), sibling]
    hub = z == i
    below = z <= i
    below_across = z <= across

    def dev(zz, yy, ii):
        return {"col": zz * 2 + yy, "row": ii}

    def remote(src, dst, ss, rr, to):
        return pltpu.make_async_remote_copy(
            src_ref=src, dst_ref=dst, send_sem=ss, recv_sem=rr, device_id=to, device_id_type=pl.DeviceIdType.MESH)

    barrier = pltpu.get_barrier_semaphore()

    def greet(to):
        pl.semaphore_signal(barrier, inc=1, device_id=to, device_id_type=pl.DeviceIdType.MESH)

    greet(dev(z, 1 - y, i))
    greet(dev(z, 1 - y, across))
    for k in range(zn):
        zz = lax.rem(z + k, zn)
        for n in range(0 if k else 1, nr):
            greet(dev(zz, y, lax.rem(i + n, nr)))
    greeted = 2 + zn * nr - 1

    def place(t):
        sent = t < 6
        k = jnp.where(sent, lax.div(t, 3), t - 6)
        kind = jnp.where(sent, lax.rem(t, 3), 3)
        return k, kind, lax.rem(y + 1 - lax.div(kind, 2), 2), lax.rem(x + 1 - lax.rem(kind, 2), 2)

    def rows_of(t):
        k, _, h, xx = place(t)
        return pl.ds(pl.multiple_of((h * nr + 2 * xx + k) * pr, pr), pr)

    def load(src, dst, sem, t):
        rows = rows_of(t)
        return pltpu.make_async_copy(src.at[rows, :], dst.at[rows, :], sem.at[t])

    def used(t):
        kind = place(t)[1]
        return jnp.logical_or(z < i, jnp.logical_and(hub, jnp.logical_or(y == 0, kind >= 2)))

    def guard(tri, cond, f):
        if tri:
            pl.when(cond)(f)
        else:
            f()

    def load_all(src, dst, sem, tri):
        @pl.loop(0, 8)
        def _(t):
            guard(tri, used(t), lambda: load(src, dst, sem, t).start())

    known = pltpu.make_async_copy(prior, priv, rsem.at[2])
    known.start()
    load_all(panel.at[0], pbuf, psem, False)

    def side(b):
        lanes = pl.ds(pl.multiple_of(y * nr * pr, nr * pr), nr * pr)
        return pltpu.make_async_copy(rs.at[b, :, lanes], rsv.at[b], rsem.at[b])

    @pl.when(hub)
    def _():
        for b in range(2):
            side(b).start()

    def halves(v):
        high = v.astype(BF16)
        return high, (v - high.astype(F32)).astype(BF16)

    known.wait()
    w0[:r, :], w0[r:, :] = halves(priv[...])

    def product(buf, w, t):
        a1, a2 = halves(buf[rows_of(t), :])
        p = lax.dot_general(w[...], a1, NT, preferred_element_type=F32)
        p = p + lax.dot_general(w[...], a2, NT, preferred_element_type=F32)
        return p[:r] + p[r:]

    def s1(ph, t, n):
        k, kind, h, xx = place(t)
        return remote(part.at[ph, t, sub[n]], r1.at[ph, t, sub[n]], s1_s.at[ph, t, n], s1_r.at[ph, t, n],
                      dev(z, h, 2 * xx + c))

    def s1_start(ph, t):
        kind = place(t)[1]
        pl.when(kind < 3)(lambda: s1(ph, t, 0).start())

        @pl.when(kind == 1)
        def _():
            for n in subs[1:]:
                s1(ph, t - 1, n).start()
                s1(ph, t, n).start()

        @pl.when(kind == 2)
        def _():
            for n in subs[1:]:
                s1(ph, t, n).start()

    def less_side(ref, b, t):
        k, kind, _, xx = place(t)

        @pl.when(jnp.logical_and(hub, kind >= 2))
        def _():
            lanes = pl.ds(pl.multiple_of((2 * xx + k) * pr, pr), pr)
            ref[...] = ref[...] - rsv[b, :, lanes]

    def s2(ph, k, own, n):
        src = part.at[ph, 6 + k, sub[n]] if own else r1.at[ph, k * 3 + 2, sub[n]]
        return remote(src, r2.at[ph, z, sub[n]], s2_s.at[ph, k, int(own), n], s2_r.at[ph, z, n],
                      dev(i if own else across, y, 2 * x + k))

    def s2_here(k, own):
        return jnp.logical_and(z == (i if own else across), c == k)

    def gather(ph, k, n, tri):
        def across_part():
            s1(ph, k * 3 + 2, n).wait_recv()
            val = r1.at[ph, k * 3 + 2, sub[n]]

            def add():
                s1(ph, k * 3, n).wait_recv()
                val[...] = val[...] + r1[ph, k * 3, sub[n]]

            guard(tri, jnp.logical_or(z < across, y == 1), add)
            here = s2_here(k, False)

            @pl.when(here)
            def _():
                r2[ph, z, sub[n]] = val[...]

            pl.when(jnp.logical_not(here))(lambda: s2(ph, k, False, n).start())

        def own_part():
            val = part.at[ph, 6 + k, sub[n]]

            def add():
                s1(ph, k * 3 + 1, n).wait_recv()
                val[...] = val[...] + r1[ph, k * 3 + 1, sub[n]]

            guard(tri, jnp.logical_or(z < i, y == 1), add)
            here = s2_here(k, True)

            @pl.when(here)
            def _():
                r2[ph, z, sub[n]] = val[...]

            pl.when(jnp.logical_not(here))(lambda: s2(ph, k, True, n).start())

        guard(tri, below, own_part)
        guard(tri, below_across, across_part)

    def s3(ph, m, n):
        there = xv.at[ph, i, sub[n]]
        return remote(there, there, s3_s.at[ph, m, n], s3_r.at[ph, i, n], dev(z, y, others[m]))

    def s3_from(ph, m, n):
        there = xv.at[ph, others[m], sub[n]]
        return remote(there, there, s3_s.at[ph, m, n], s3_r.at[ph, others[m], n], dev(z, y, others[m]))

    def at_out(b, yy, q, n):
        return out.at[b, sub[n], pl.ds(pl.multiple_of((yy * nr + q) * pr, pr), pr)]

    def publish(b, ph, k, n):
        return remote(xv.at[ph, i, sub[n]], at_out(b, y, i, n), o_s.at[b, k, n], o_r.at[b, i, n],
                      dev(lax.rem(z + k, zn), y, z))

    def published(b, ph, q, n):
        return remote(xv.at[ph, i, sub[n]], at_out(b, y, q, n), o_s.at[b, 0, n], o_r.at[b, q, n], dev(i, y, q))

    def relay(k, n):
        return remote(xv.at[1, i, sub[n]], lead.at[z, sub[n]], l_s.at[k, n], l_r.at[z, n], dev(lax.rem(z + k, zn), y, i))

    def relayed(zz, n):
        return remote(lead.at[zz, sub[n]], lead.at[zz, sub[n]], l_s.at[0, n], l_r.at[zz, n], dev(zz, y, i))

    def deliver(j, n):
        return remote(lead.at[j, sub[n]], at_out(0, y, i, n), o_s.at[0, j, n], o_r.at[0, i, n], dev(z, y, j))

    def relay_all():
        lead[z] = xv[1, i]
        for n in subs:
            for k in (2, 1, 3):
                relay(k, n).start()

    def deliver_all():
        for n in subs:
            for j in range(nr):
                pl.when(z != j)(lambda j=j, n=n: relayed(j, n).wait_recv())
                pl.when(i != j)(lambda j=j, n=n: deliver(j, n).start())

                @pl.when(i == j)
                def _(j=j, n=n):
                    at_out(0, y, i, n)[...] = lead[j, sub[n]]

    def here(b, q):
        return i == q if b == 0 else jnp.logical_and(hub, i == q)

    def pass_on(b, q, n, yy):
        return remote(at_out(b, yy, q, n), at_out(b, yy, q, n), f_s.at[b, q, n], f_r.at[b, q, n], dev(z, 1 - y, i))

    def finish(ph, n, tri, sign, b):
        mine = lax.rem(z, 2) == c
        for zz in range(zn):
            def arrive(zz=zz):
                away = jnp.logical_not(jnp.logical_and(z == zz, mine))
                pl.when(away)(lambda: remote(
                    r2.at[ph, zz, sub[n]], r2.at[ph, zz, sub[n]], s2_s.at[ph, 0, 0, n], s2_r.at[ph, zz, n],
                    dev(zz, y, sibling)).wait_recv())
                val = r2[ph, zz, sub[n]]
                val = val if sign > 0 else -val
                xv[ph, i, sub[n]] = val if zz == 0 else xv[ph, i, sub[n]] + val

            guard(tri and zz > 0, zz <= z, arrive)
        if ph < 3:
            for m in range(3):
                s3(ph, m, n).start()
        if b == 1:
            for k in range(1, zn):
                publish(b, ph, k, n).start()
            pl.when(jnp.logical_not(hub))(lambda: publish(b, ph, 0, n).start())

            @pl.when(hub)
            def _():
                at_out(b, y, i, n)[...] = xv[ph, i, sub[n]]

    def reduce(ph, tri, sign, b=None, between=None):
        for n in subs:
            gather(ph, 0, n, tri)
        for n in subs:
            pl.when(c == 0)(lambda n=n: finish(ph, n, tri, sign, b))
            gather(ph, 1, n, tri)
        if between is not None:
            between()
        for n in subs:
            pl.when(c == 1)(lambda n=n: finish(ph, n, tri, sign, b))

    def drain(ph, tri):
        for k in range(2):
            for n in subs:
                for kind in range(3):
                    t = k * 3 + kind
                    guard(tri, used(t), lambda t=t, n=n: s1(ph, t, n).wait_send())
                for own, cond in ((True, below), (False, below_across)):
                    live = jnp.logical_not(s2_here(k, own))
                    if tri:
                        live = jnp.logical_and(live, cond)
                    pl.when(live)(lambda k=k, n=n, own=own: s2(ph, k, own, n).wait_send())

    def spread(ph):
        def put(q, n):
            lanes = pl.ds(pl.multiple_of(q * pr, pr), pr)
            wv[sub[n], lanes], wv[low[n], lanes] = halves(xv[ph, q, sub[n]])

        for n in subs:
            put(i, n)
        for m in (2, 0, 1):
            for n in subs:
                s3_from(ph, m, n).wait_recv()
                put(others[m], n)

    def spread_end(ph):
        for m in range(3):
            for n in subs:
                s3(ph, m, n).wait_send()

    def hand_over(b, ph):
        for q in (0, 2, 1, 3):
            for n in subs:
                pl.when(jnp.logical_not(here(b, q)))(lambda q=q, n=n: published(b, ph, q, n).wait_recv())
                pass_on(b, q, n, y).start()

    def hand_over_end(b, ph):
        for n in subs:
            if b == 1:
                for k in range(1, zn):
                    publish(b, ph, k, n).wait_send()
                pl.when(jnp.logical_not(hub))(lambda n=n: publish(b, ph, 0, n).wait_send())
            else:
                for k in range(1, zn):
                    relay(k, n).wait_send()
                for j in range(nr):
                    pl.when(i != j)(lambda j=j, n=n: deliver(j, n).wait_send())
            for q in range(nr):
                pass_on(b, q, n, y).wait_send()
                pass_on(b, q, n, 1 - y).wait_recv()

    def multiply(ph, src, buf, sem, w, tri, after=None, more=False):
        @pl.loop(0, 8)
        def _(t):
            def piece():
                load(src, buf, sem, t).wait()
                val = product(buf, w, t)
                if more:
                    val = val + part1[t]
                part[ph, t] = val
                s1_start(ph, t)
                if after is not None:
                    load(after, buf, sem, t).start()

            guard(tri, used(t), piece)

    @pl.loop(0, 8)
    def _(t):
        load(panel.at[0], pbuf, psem, t).wait()
        part[0, t] = product(pbuf, w0, t)
        load(panel.at[1], pbuf, psem, t).start()

    @pl.when(hub)
    def _():
        for b in range(2):
            side(b).wait()
        pl.loop(0, 8)(lambda t: less_side(part.at[0, t], 0, t))

    pl.semaphore_wait(barrier, greeted)
    for k in range(2):
        for n in subs:
            for kind in range(3):
                s1(0, k * 3 + kind, n).start()
    load_all(inv.at[0], buf0, sem0, True)

    @pl.loop(0, 8)
    def _(t):
        load(panel.at[1], pbuf, psem, t).wait()
        part1[t] = product(pbuf, w0, t)
        less_side(part1.at[t], 1, t)

    load_all(coup, buf1, sem1, False)
    reduce(0, False, -1)
    drain(0, False)
    spread(0)
    multiply(1, inv.at[0], buf0, sem0, wv, True, after=inv.at[1])
    reduce(1, True, 1, 0)
    drain(1, True)
    spread(1)
    relay_all()
    multiply(2, coup, buf1, sem1, wv, False, more=True)
    reduce(2, False, -1, between=deliver_all)
    drain(2, False)
    spread(2)
    multiply(3, inv.at[1], buf0, sem0, wv, True)
    reduce(3, True, 1, 1, between=lambda: hand_over(0, 1))
    hand_over(1, 3)
    drain(3, True)
    for ph in range(3):
        spread_end(ph)
    hand_over_end(0, 1)
    hand_over_end(1, 3)


def paired_call(panel, prior, side, coupling, inverses):
    rows, width = coupling.shape
    r = prior.shape[1]
    pr = rows // 8
    dma = pltpu.SemaphoreType.DMA
    hbm = pl.BlockSpec(memory_space=pl.ANY)
    vmem = pl.BlockSpec(memory_space=pltpu.VMEM)
    return pl.pallas_call(
        paired,
        out_shape=jax.ShapeDtypeStruct(side.shape, F32),
        in_specs=[hbm, hbm, hbm, hbm, hbm],
        out_specs=vmem,
        scratch_shapes=[
            pltpu.VMEM((4, 8, r, pr), F32),
            pltpu.VMEM((8, r, pr), F32),
            pltpu.VMEM((4, 6, r, pr), F32),
            pltpu.VMEM((4, 4, r, pr), F32),
            pltpu.VMEM((4, 4, r, pr), F32),
            pltpu.VMEM((2 * r, width), BF16),
            pltpu.VMEM((2 * r, prior.shape[0]), BF16),
            pltpu.VMEM(panel.shape[1:], F32),
            pltpu.VMEM((rows, width), F32),
            pltpu.VMEM((rows, width), F32),
            pltpu.VMEM((2, r, 4 * pr), F32),
            pltpu.VMEM((r, prior.shape[0]), F32),
            pltpu.VMEM((4, r, pr), F32),
            dma((8,)), dma((8,)), dma((8,)), dma((3,)),
            dma((4, 6, SUBS)), dma((4, 6, SUBS)),
            dma((4, 2, 2, SUBS)), dma((4, 4, SUBS)),
            dma((3, 3, SUBS)), dma((3, 4, SUBS)),
            dma((2, 4, SUBS)), dma((2, 4, SUBS)),
            dma((2, 4, SUBS)), dma((2, 4, SUBS)),
            dma((4, SUBS)), dma((4, SUBS)),
        ],
        compiler_params=pltpu.CompilerParams(collective_id=0, has_side_effects=True, vmem_limit_bytes=67043328),
    )(panel, prior.T, side, coupling, inverses)


def shards(nc, nr, panel, prior, right_side, coupling, inverses):
    q = nc // nr
    rows, width = coupling.shape
    r = prior.shape[1]
    pr = rows // nc
    dense = pr % 128 == 0
    lanes = 2 * r
    dma = pltpu.SemaphoreType.DMA
    hbm = pl.BlockSpec(memory_space=pl.ANY)
    vmem = pl.BlockSpec(memory_space=pltpu.VMEM)
    side = right_side.transpose(0, 2, 1)
    if nc == 8 and nr == 4 and dense:
        return paired_call(panel, prior, side, coupling, inverses).transpose(0, 2, 1)
    if not dense:
        side = side.reshape(2, r, nc, pr).transpose(0, 2, 1, 3)
    solved = pl.pallas_call(
        functools.partial(kernel, q, nr),
        out_shape=jax.ShapeDtypeStruct(side.shape, F32),
        in_specs=[hbm, vmem, hbm, hbm, hbm],
        out_specs=vmem,
        scratch_shapes=[
            pltpu.VMEM((q, nr, r, pr), F32),
            pltpu.VMEM((q, nr, r, pr), F32),
            pltpu.VMEM((4, q - 1, nr, r, pr), F32),
            pltpu.VMEM((4, nr - 1, r, pr), F32),
            pltpu.VMEM((4, r, pr), F32),
            pltpu.VMEM((3, nr, r, pr), F32),
            pltpu.VMEM((width, lanes), BF16),
            pltpu.VMEM((prior.shape[0], lanes), BF16),
            pltpu.VMEM(panel.shape[1:], F32),
            pltpu.VMEM((rows, width), F32),
            pltpu.VMEM((rows, width), F32),
            pltpu.VMEM((2, r, pr), F32),
            dma((nc,)), dma((nc,)), dma((nc,)), dma((2,)),
            dma((4, q - 1, nr, SUBS)), dma((4, q - 1, nr, SUBS)),
            dma((4, nr - 1, SUBS)), dma((4, nr - 1, SUBS)),
            dma((3, nr // 2, SUBS)), dma((3, nr, SUBS)), dma((3, nr, SUBS)),
            dma((2, nr - 1, SUBS)), dma((2, nr - 1, SUBS)),
            dma((2, q - 1, nr, SUBS)), dma((2, q - 1, nr, SUBS)),
        ],
        compiler_params=pltpu.CompilerParams(collective_id=0, has_side_effects=True, vmem_limit_bytes=67043328),
    )(panel, prior.T, side, coupling, inverses)
    if not dense:
        solved = solved.transpose(0, 2, 1, 3).reshape(2, r, rows)
    return solved.transpose(0, 2, 1)


def solution(mesh):
    in_specs = (
        P(None, "row", "col"),
        P("col", None),
        P(None, "row", None),
        P("row", "col"),
        P(None, "row", "col"),
    )
    out_specs = P(None, "row", None)
    body = functools.partial(shards, mesh.shape["col"], mesh.shape["row"])
    return jax.shard_map(body, mesh=mesh, in_specs=in_specs, out_specs=out_specs, check_vma=False)
```

```python
import functools
import jax
import jax.numpy as jnp
from jax import lax
from jax.experimental import pallas as pl
from jax.experimental.pallas import tpu as pltpu
from jax.sharding import PartitionSpec as P

F32, BF16 = jnp.float32, jnp.bfloat16
SUBS = 2
NT = (((1,), (1,)), ((), ()))


def kernel(q, nr, panel, prior, rs, coup, inv, out, part, part1, ra, rb, tv, xv, wv, w0, pbuf, buf0, buf1, rsv,
           psem, sem0, sem1, rsem, a_s, a_r, b_s, b_r, c1_s, x_r, c2_s, d_s, d_r, dy_s, dy_r):
    zn = nr
    nx = nr // 2
    r, pr = part.shape[2:]
    subs = range(SUBS)
    sub = [pl.ds(h * (r // SUBS), r // SUBS) for h in subs]
    col = lax.axis_index("col")
    i = lax.axis_index("row")
    z, y = lax.div(col, q), lax.rem(col, q)
    below = z <= i
    hub = z == i
    direct = lax.rem(i, 2) == lax.rem(z, 2)
    far = jnp.logical_and(direct, jnp.logical_not(hub))
    sibling = i + 1 - 2 * lax.rem(i, 2)

    def dev(zz, yy, ii):
        return {"col": zz * q + yy, "row": ii}

    def zfwd(k):
        return lax.rem(z + 1 + k, zn)

    def zback(k):
        return lax.rem(z + zn - 1 - k, zn)

    def yfwd(m):
        return lax.rem(y + 1 + m, q)

    def yback(m):
        return lax.rem(y + q - 1 - m, q)

    def remote(src, dst, ss, rr, to):
        return pltpu.make_async_remote_copy(
            src_ref=src, dst_ref=dst, send_sem=ss, recv_sem=rr, device_id=to, device_id_type=pl.DeviceIdType.MESH)

    def rows_of(m, k):
        return pl.ds(pl.multiple_of((yfwd(m) * zn + zfwd(k)) * pr, pr), pr)

    def load(src, dst, sem, m, k):
        rows = rows_of(m, k)
        return pltpu.make_async_copy(src.at[rows, :], dst.at[rows, :], sem.at[m * zn + k])

    def load_all(src, dst, sem):
        for m in range(q):
            pl.loop(0, zn)(lambda k, m=m: load(src, dst, sem, m, k).start())

    load_all(panel.at[0], pbuf, psem)

    def piece(ref, b, yy, zz):
        if len(ref.shape) == 4:
            return ref.at[b, yy * zn + zz]
        return ref.at[b, :, pl.ds(pl.multiple_of((yy * zn + zz) * pr, pr), pr)]

    rs_copies = [pltpu.make_async_copy(piece(rs, b, y, z), rsv.at[b], rsem.at[b]) for b in range(2)]
    for c in rs_copies:
        c.start()
    pl.when(below)(lambda: load_all(inv.at[0], buf0, sem0))

    barrier = pltpu.get_barrier_semaphore()
    for k in range(zn - 1):
        pl.semaphore_signal(barrier, inc=1, device_id=dev(zfwd(k), y, i), device_id_type=pl.DeviceIdType.MESH)
    for m in range(q - 1):
        pl.semaphore_signal(barrier, inc=1, device_id=dev(z, yfwd(m), i), device_id_type=pl.DeviceIdType.MESH)
    for n in range(nr - 1):
        pl.semaphore_signal(barrier, inc=1, device_id=dev(z, y, lax.rem(i + 1 + n, nr)), device_id_type=pl.DeviceIdType.MESH)

    @pl.when(far)
    def _():
        for k in range(zn):
            pl.semaphore_signal(barrier, inc=1, device_id=dev(k, y, z), device_id_type=pl.DeviceIdType.MESH)

    def split(x):
        high = x.astype(BF16).astype(F32)
        return jnp.concatenate([high, x - high], axis=0).T.astype(BF16)

    w0[...] = split(prior[...])
    for c in rs_copies:
        c.wait()
    pl.semaphore_wait(barrier, zn - 1 + q - 1 + nr - 1 + nx - 1)

    def product(buf, w, m, k):
        a = buf[rows_of(m, k), :]
        a1 = a.astype(BF16)
        a2 = (a - a1.astype(F32)).astype(BF16)
        p = jnp.dot(jnp.concatenate([a1, a2], axis=0), w[...], preferred_element_type=F32)
        s = (p[:pr] + p[pr:]).T
        return s[:r] + s[r:]

    def a_copy(ph, m, k, h):
        return remote(part.at[yfwd(m), zfwd(k), sub[h]], ra.at[ph, m, k, sub[h]], a_s.at[ph, m, k, h],
                      a_r.at[ph, m, k, h], dev(z, yfwd(m), i))

    def b_copy(ph, k, h):
        return remote(part.at[y, zfwd(k), sub[h]], rb.at[ph, k, sub[h]], b_s.at[ph, k, h], b_r.at[ph, k, h],
                      dev(zfwd(k), y, i))

    def guard(tri, cond, f):
        if tri:
            pl.when(cond)(f)
        else:
            f()

    def reduce(ph, src, buf, sem, w, tri, rhs, emit, add=False, after=None):
        def absorb(k, h):
            val = part[y, zfwd(k), sub[h]]
            for m in range(q - 1):
                a_copy(ph, m, k, h).wait_recv()
                val = val + ra[ph, m, k, sub[h]]
            part[y, zfwd(k), sub[h]] = val
            pl.when(k < zn - 1)(lambda: b_copy(ph, k, h).start())

        def compute():
            for m in range(q):
                @pl.loop(0, zn)
                def _(k):
                    load(src, buf, sem, m, k).wait()
                    val = product(buf, w, m, k)
                    if add:
                        val = val + part1[yfwd(m), zfwd(k)]
                    part[yfwd(m), zfwd(k)] = val
                    if after is not None:
                        load(after, buf, sem, m, k).start()
                    if m < q - 1:
                        a_copy(ph, m, k, 0).start()
                    else:
                        absorb(k, 0)

                if m < q - 1:
                    for h in subs[1:]:
                        pl.loop(0, zn)(lambda k, m=m, h=h: a_copy(ph, m, k, h).start())
            for h in subs[1:]:
                pl.loop(0, zn)(lambda k, h=h: absorb(k, h))

        guard(tri, below, compute)
        if tri:
            @pl.when(jnp.logical_not(below))
            def _():
                part[y, z] = jnp.zeros((r, pr), F32)
        for h in subs:
            for k in range(zn - 1):
                def take(k=k):
                    b_copy(ph, k, h).wait_recv()
                    part[y, z, sub[h]] = part[y, z, sub[h]] + rb[ph, k, sub[h]]

                guard(tri, zback(k) <= i, take)
            val = part[y, z, sub[h]]
            tv[ph, sub[h]] = val if rhs is None else rsv[rhs, sub[h]] - val
            emit(ph, h)

    def drain(ph, tri):
        def waits():
            for h in subs:
                for m in range(q - 1):
                    pl.loop(0, zn)(lambda k, m=m: a_copy(ph, m, k, h).wait_send())
                pl.loop(0, zn - 1)(lambda k: b_copy(ph, k, h).wait_send())

        guard(tri, below, waits)

    def up(ph, n, h):
        return remote(tv.at[ph, sub[h]], xv.at[ph, z, sub[h]], c1_s.at[ph, n, h], x_r.at[ph, z, h],
                      dev(i, y, lax.rem(i + 2 * n, nr)))

    def fwd(ph, s, h):
        there = xv.at[ph, s, sub[h]]
        return remote(there, there, c2_s.at[ph, s, h], x_r.at[ph, s, h], dev(z, y, sibling))

    def rise(ph, h):
        @pl.when(hub)
        def _():
            xv[ph, z, sub[h]] = tv[ph, sub[h]]

        for n in range(1, nx):
            up(ph, n, h).start()
        pl.when(jnp.logical_not(hub))(lambda: up(ph, 0, h).start())

    def spread(ph):
        for h in subs:
            @pl.loop(0, zn)
            def _(k):
                s = lax.rem(z + k, zn)
                pl.when(jnp.logical_not(jnp.logical_and(hub, s == z)))(lambda: fwd(ph, s, h).wait_recv())
                pl.when(direct)(lambda: fwd(ph, s, h).start())
                if h == SUBS - 1:
                    wv[pl.ds(pl.multiple_of(s * pr, pr), pr), :] = split(xv[ph, s])

    def spread_end(ph):
        for h in subs:
            for n in range(1, nx):
                up(ph, n, h).wait_send()
            pl.when(jnp.logical_not(hub))(lambda: up(ph, 0, h).wait_send())
            pl.when(direct)(lambda: pl.loop(0, zn)(lambda s: fwd(ph, s, h).wait_send()))

    def at_out(b, yy, zz, h):
        return piece(out, b, yy, zz).at[sub[h]]

    def dz_copy(b, ph, k, h, zz):
        return remote(tv.at[ph, sub[h]], at_out(b, y, zz, h), d_s.at[b, k, h], d_r.at[b, k, h], dev(zfwd(k), y, i))

    def dy_copy(b, m, slot, s, h, yy):
        return remote(at_out(b, y, s, h), at_out(b, yy, s, h), dy_s.at[b, m, slot, h], dy_r.at[b, m, slot, h],
                      dev(z, yfwd(m), i))

    def publish_z(b, ph, h):
        at_out(b, y, z, h)[...] = tv[ph, sub[h]]
        for k in range(zn - 1):
            dz_copy(b, ph, k, h, z).start()

    def publish_own(b, h):
        for m in range(q - 1):
            dy_copy(b, m, 0, z, h, y).start()

    def publish_y(b, ph, h):
        for k in range(zn - 1):
            dz_copy(b, ph, k, h, zback(k)).wait_recv()
            for m in range(q - 1):
                dy_copy(b, m, k + 1, zback(k), h, y).start()

    def publish_end(b, ph):
        for h in subs:
            for slot in range(zn):
                s = z if slot == 0 else zback(slot - 1)
                for m in range(q - 1):
                    dy_copy(b, m, slot, s, h, yback(m)).wait_recv()
                    dy_copy(b, m, slot, s, h, y).wait_send()
            for k in range(zn - 1):
                dz_copy(b, ph, k, h, z).wait_send()

    def second_carried():
        for m in range(q):
            @pl.loop(0, zn)
            def _(k):
                load(panel.at[1], pbuf, psem, m, k).wait()
                part1[yfwd(m), zfwd(k)] = product(pbuf, w0, m, k)

    def last(ph, h):
        publish_z(1, ph, h)
        publish_own(1, h)

    reduce(0, panel.at[0], pbuf, psem, w0, False, 0, rise, after=panel.at[1])
    second_carried()
    load_all(coup, buf1, sem1)
    spread(0)
    drain(0, False)
    reduce(1, inv.at[0], buf0, sem0, wv, True, None, rise, after=inv.at[1])
    spread(1)
    drain(1, True)
    publish_z(0, 1, 0)
    reduce(2, coup, buf1, sem1, wv, False, 1, rise, add=True)
    publish_own(0, 0)
    publish_y(0, 1, 0)
    spread(2)
    drain(2, False)
    for h in subs[1:]:
        publish_z(0, 1, h)
        publish_own(0, h)
    reduce(3, inv.at[1], buf0, sem0, wv, True, None, last)
    for h in subs[1:]:
        publish_y(0, 1, h)
    for h in subs:
        publish_y(1, 3, h)
    drain(3, True)
    for ph in range(3):
        spread_end(ph)
    publish_end(0, 1)
    publish_end(1, 3)


def paired(panel, prior, rs, coup, inv, out, part, part1, r1, r2, xv, wv, w0, pbuf, buf0, buf1, rsv, priv, lead,
           psem, sem0, sem1, rsem, s1_s, s1_r, s2_s, s2_r, s3_s, s3_r, o_s, o_r, f_s, f_r, l_s, l_r):
    zn = nr = 4
    kinds = 4
    r, pr = part.shape[2:]
    subs = range(SUBS)
    sub = [pl.ds(n * (r // SUBS), r // SUBS) for n in subs]
    low = [pl.ds(r + n * (r // SUBS), r // SUBS) for n in subs]
    col = lax.axis_index("col")
    i = lax.axis_index("row")
    z, y = lax.div(col, 2), lax.rem(col, 2)
    x, c = lax.div(i, 2), lax.rem(i, 2)
    across = lax.rem(i + 2, nr)
    sibling = i + 1 - 2 * c
    others = [across, lax.rem(sibling + 2, nr), sibling]
    hub = z == i
    below = z <= i
    below_across = z <= across

    def dev(zz, yy, ii):
        return {"col": zz * 2 + yy, "row": ii}

    def remote(src, dst, ss, rr, to):
        return pltpu.make_async_remote_copy(
            src_ref=src, dst_ref=dst, send_sem=ss, recv_sem=rr, device_id=to, device_id_type=pl.DeviceIdType.MESH)

    barrier = pltpu.get_barrier_semaphore()

    def greet(to):
        pl.semaphore_signal(barrier, inc=1, device_id=to, device_id_type=pl.DeviceIdType.MESH)

    greet(dev(z, 1 - y, i))
    greet(dev(z, 1 - y, across))
    for k in (2, 3, 1, 0):
        zz = lax.rem(z + k, zn)
        for n in range(0 if k else 1, nr):
            greet(dev(zz, y, lax.rem(i + n, nr)))
    greeted = 2 + zn * nr - 1

    def place(t):
        k, kind = lax.div(t, kinds), lax.rem(t, kinds)
        return k, kind, lax.rem(y + 1 - lax.div(kind, 2), 2), lax.rem(x + 1 - lax.rem(kind, 2), 2)

    def rows_of(t):
        k, _, h, xx = place(t)
        return pl.ds(pl.multiple_of((h * nr + 2 * xx + k) * pr, pr), pr)

    def load(src, dst, sem, t):
        rows = rows_of(t)
        return pltpu.make_async_copy(src.at[rows, :], dst.at[rows, :], sem.at[t])

    def used(t):
        kind = lax.rem(t, kinds)
        return jnp.logical_or(z < i, jnp.logical_and(hub, jnp.logical_or(y == 0, kind >= 2)))

    def guard(tri, cond, f):
        if tri:
            pl.when(cond)(f)
        else:
            f()

    def load_all(src, dst, sem, tri):
        @pl.loop(0, 2 * kinds)
        def _(t):
            guard(tri, used(t), lambda: load(src, dst, sem, t).start())

    known = pltpu.make_async_copy(prior, priv, rsem.at[2])
    known.start()
    load_all(panel.at[0], pbuf, psem, False)

    def side(b):
        lanes = pl.ds(pl.multiple_of(y * nr * pr, nr * pr), nr * pr)
        return pltpu.make_async_copy(rs.at[b, :, lanes], rsv.at[b], rsem.at[b])

    @pl.when(hub)
    def _():
        for b in range(2):
            side(b).start()

    def halves(v):
        high = v.astype(BF16)
        return high, (v - high.astype(F32)).astype(BF16)

    known.wait()
    w0[:r, :], w0[r:, :] = halves(priv[...])

    def product(buf, w, t):
        a1, a2 = halves(buf[rows_of(t), :])
        p = lax.dot_general(w[...], a1, NT, preferred_element_type=F32)
        p = p + lax.dot_general(w[...], a2, NT, preferred_element_type=F32)
        return p[:r] + p[r:]

    def s1(ph, t, n):
        k, kind, h, xx = place(t)
        slot = k * 3 + kind
        return remote(part.at[ph, t, sub[n]], r1.at[ph, slot, sub[n]], s1_s.at[ph, slot, n], s1_r.at[ph, slot, n],
                      dev(z, h, 2 * xx + c))

    def s1_start(ph, t):
        @pl.when(lax.rem(t, kinds) < 3)
        def _():
            for n in subs:
                s1(ph, t, n).start()

    def less_side(ref, b, t):
        k, kind, _, xx = place(t)

        @pl.when(jnp.logical_and(hub, kind >= 2))
        def _():
            lanes = pl.ds(pl.multiple_of((2 * xx + k) * pr, pr), pr)
            ref[...] = ref[...] - rsv[b, :, lanes]

    def s2(ph, k, own, n):
        src = part.at[ph, k * kinds + 3, sub[n]] if own else r1.at[ph, k * 3 + 2, sub[n]]
        return remote(src, r2.at[ph, z, sub[n]], s2_s.at[ph, k, int(own), n], s2_r.at[ph, z, n],
                      dev(i if own else across, y, 2 * x + k))

    def s2_here(k, own):
        return jnp.logical_and(z == (i if own else across), c == k)

    def gather(ph, k, n, tri, own):
        row = i if own else across
        slot = k * 3 + (1 if own else 0)
        val = part.at[ph, k * kinds + 3, sub[n]] if own else r1.at[ph, k * 3 + 2, sub[n]]

        def collect():
            if not own:
                s1(ph, k * kinds + 2, n).wait_recv()

            def add():
                s1(ph, slot - k * 3 + k * kinds, n).wait_recv()
                val[...] = val[...] + r1[ph, slot, sub[n]]

            guard(tri, jnp.logical_or(z < row, y == 1), add)
            here = s2_here(k, own)

            @pl.when(here)
            def _():
                r2[ph, z, sub[n]] = val[...]

            pl.when(jnp.logical_not(here))(lambda: s2(ph, k, own, n).start())

        guard(tri, z <= row, collect)

    def s3(ph, m, n):
        there = xv.at[ph, i, sub[n]]
        return remote(there, there, s3_s.at[ph, m, n], s3_r.at[ph, i, n], dev(z, y, others[m]))

    def s3_from(ph, m, n):
        there = xv.at[ph, others[m], sub[n]]
        return remote(there, there, s3_s.at[ph, m, n], s3_r.at[ph, others[m], n], dev(z, y, others[m]))

    def at_out(b, yy, q, n):
        return out.at[b, sub[n], pl.ds(pl.multiple_of((yy * nr + q) * pr, pr), pr)]

    def publish(b, ph, k, n):
        return remote(xv.at[ph, i, sub[n]], at_out(b, y, i, n), o_s.at[b, k, n], o_r.at[b, i, n],
                      dev(lax.rem(z + k, zn), y, z))

    def published(b, ph, q, n):
        return remote(xv.at[ph, i, sub[n]], at_out(b, y, q, n), o_s.at[b, 0, n], o_r.at[b, q, n], dev(i, y, q))

    def relay(k, n):
        return remote(xv.at[1, i, sub[n]], lead.at[z, sub[n]], l_s.at[k, n], l_r.at[z, n], dev(lax.rem(z + k, zn), y, i))

    def relayed(zz, n):
        return remote(lead.at[zz, sub[n]], lead.at[zz, sub[n]], l_s.at[0, n], l_r.at[zz, n], dev(zz, y, i))

    def deliver(j, n):
        return remote(lead.at[j, sub[n]], at_out(0, y, i, n), o_s.at[0, j, n], o_r.at[0, i, n], dev(z, y, j))

    def relay_all():
        lead[z] = xv[1, i]
        for n in subs:
            for k in (2, 1, 3):
                relay(k, n).start()

    def deliver_all():
        for n in subs:
            for j in range(nr):
                pl.when(z != j)(lambda j=j, n=n: relayed(j, n).wait_recv())
                pl.when(i != j)(lambda j=j, n=n: deliver(j, n).start())

                pl.when(i == j)(lambda j=j, n=n: keep(0, 1, n).start())

    def keep(b, ph, n):
        src = lead.at[i, sub[n]] if b == 0 else xv.at[ph, i, sub[n]]
        return pltpu.make_async_copy(src, at_out(b, y, i, n), o_r.at[b, i, n])

    def here(b, q):
        return i == q if b == 0 else jnp.logical_and(hub, i == q)

    def pass_on(b, q, n, yy):
        return remote(at_out(b, yy, q, n), at_out(b, yy, q, n), f_s.at[b, q, n], f_r.at[b, q, n], dev(z, 1 - y, i))

    def finish(ph, n, tri, sign, b):
        mine = lax.rem(z, 2) == c
        for zz in range(zn):
            def arrive(zz=zz):
                away = jnp.logical_not(jnp.logical_and(z == zz, mine))
                pl.when(away)(lambda: remote(
                    r2.at[ph, zz, sub[n]], r2.at[ph, zz, sub[n]], s2_s.at[ph, 0, 0, n], s2_r.at[ph, zz, n],
                    dev(zz, y, sibling)).wait_recv())
                val = r2[ph, zz, sub[n]]
                val = val if sign > 0 else -val
                xv[ph, i, sub[n]] = val if zz == 0 else xv[ph, i, sub[n]] + val

            guard(tri and zz > 0, zz <= z, arrive)
        if ph < 3:
            for m in range(3):
                s3(ph, m, n).start()
        if b == 1:
            for k in (2, 3, 1):
                publish(b, ph, k, n).start()
            pl.when(jnp.logical_not(hub))(lambda: publish(b, ph, 0, n).start())

            pl.when(hub)(lambda: keep(b, ph, n).start())

    def reduce(ph, tri, sign, b=None, between=None):
        for n in subs:
            pl.when(c == 0)(lambda n=n: finish(ph, n, tri, sign, b))
            gather(ph, 1, n, tri, True)
            gather(ph, 1, n, tri, False)
        if between is not None:
            between()
        for n in subs:
            pl.when(c == 1)(lambda n=n: finish(ph, n, tri, sign, b))

    def drain(ph, tri):
        for k in range(2):
            for n in subs:
                for kind in range(3):
                    t = k * kinds + kind
                    guard(tri, used(t), lambda t=t, n=n: s1(ph, t, n).wait_send())
                for own, cond in ((True, below), (False, below_across)):
                    live = jnp.logical_not(s2_here(k, own))
                    if tri:
                        live = jnp.logical_and(live, cond)
                    pl.when(live)(lambda k=k, n=n, own=own: s2(ph, k, own, n).wait_send())

    def spread(ph):
        def put(q, n):
            lanes = pl.ds(pl.multiple_of(q * pr, pr), pr)
            wv[sub[n], lanes], wv[low[n], lanes] = halves(xv[ph, q, sub[n]])

        for n in subs:
            put(i, n)
        for m in (2, 0, 1):
            for n in subs:
                s3_from(ph, m, n).wait_recv()
                put(others[m], n)

    def spread_end(ph):
        for m in range(3):
            for n in subs:
                s3(ph, m, n).wait_send()

    def hand_over(b, ph):
        for q in (0, 2, 1, 3):
            for n in subs:
                pl.when(jnp.logical_not(here(b, q)))(lambda q=q, n=n: published(b, ph, q, n).wait_recv())
                pl.when(here(b, q))(lambda n=n: keep(b, ph, n).wait())
                pass_on(b, q, n, y).start()

    def sent_end(b, ph):
        for n in subs:
            if b == 1:
                for k in range(1, zn):
                    publish(b, ph, k, n).wait_send()
                pl.when(jnp.logical_not(hub))(lambda n=n: publish(b, ph, 0, n).wait_send())
            else:
                for k in range(1, zn):
                    relay(k, n).wait_send()
                for j in range(nr):
                    pl.when(i != j)(lambda j=j, n=n: deliver(j, n).wait_send())

    def hand_over_end(b, ph):
        for n in subs:
            for q in range(nr):
                pass_on(b, q, n, y).wait_send()
                pass_on(b, q, n, 1 - y).wait_recv()

    def multiply(ph, src, buf, sem, w, tri, after=None, more=False):
        @pl.loop(0, 2 * kinds)
        def _(t):
            def piece():
                load(src, buf, sem, t).wait()
                val = product(buf, w, t)
                if more:
                    val = val + part1[t]
                part[ph, t] = val
                s1_start(ph, t)
                if after is not None:
                    load(after, buf, sem, t).start()

            guard(tri, used(t), piece)
            for n in subs:
                pl.when(t == kinds + 2 + n)(lambda n=n: gather(ph, 0, n, tri, True))
                pl.when(t == kinds + 2 + n)(lambda n=n: gather(ph, 0, n, tri, False))

    @pl.loop(0, 2 * kinds)
    def _(t):
        load(panel.at[0], pbuf, psem, t).wait()
        part[0, t] = product(pbuf, w0, t)
        load(panel.at[1], pbuf, psem, t).start()

    @pl.when(hub)
    def _():
        for b in range(2):
            side(b).wait()
        pl.loop(0, 2 * kinds)(lambda t: less_side(part.at[0, t], 0, t))

    pl.semaphore_wait(barrier, greeted)
    for k in range(2):
        for n in subs:
            for kind in range(3):
                s1(0, k * kinds + kind, n).start()
    load_all(inv.at[0], buf0, sem0, True)

    @pl.loop(0, 2 * kinds)
    def _(t):
        load(panel.at[1], pbuf, psem, t).wait()
        part1[t] = product(pbuf, w0, t)
        less_side(part1.at[t], 1, t)

    load_all(coup, buf1, sem1, False)
    for n in subs:
        for own in (True, False):
            gather(0, 0, n, False, own)
    reduce(0, False, -1)
    drain(0, False)
    spread(0)
    multiply(1, inv.at[0], buf0, sem0, wv, True, after=inv.at[1])
    reduce(1, True, 1, 0)
    drain(1, True)
    spread(1)
    relay_all()
    multiply(2, coup, buf1, sem1, wv, False, more=True)
    reduce(2, False, -1, between=deliver_all)
    drain(2, False)
    spread(2)
    multiply(3, inv.at[1], buf0, sem0, wv, True)
    reduce(3, True, 1, 1, between=lambda: hand_over(0, 1))
    drain(3, True)
    for ph in range(3):
        spread_end(ph)
    sent_end(0, 1)
    hand_over(1, 3)
    hand_over_end(0, 1)
    sent_end(1, 3)
    hand_over_end(1, 3)


def paired_call(panel, prior, side, coupling, inverses):
    rows, width = coupling.shape
    r = prior.shape[1]
    pr = rows // 8
    dma = pltpu.SemaphoreType.DMA
    hbm = pl.BlockSpec(memory_space=pl.ANY)
    return pl.pallas_call(
        paired,
        out_shape=jax.ShapeDtypeStruct(side.shape, F32),
        in_specs=[hbm, hbm, hbm, hbm, hbm],
        out_specs=hbm,
        scratch_shapes=[
            pltpu.VMEM((4, 8, r, pr), F32),
            pltpu.VMEM((8, r, pr), F32),
            pltpu.VMEM((4, 6, r, pr), F32),
            pltpu.VMEM((4, 4, r, pr), F32),
            pltpu.VMEM((4, 4, r, pr), F32),
            pltpu.VMEM((2 * r, width), BF16),
            pltpu.VMEM((2 * r, prior.shape[0]), BF16),
            pltpu.VMEM(panel.shape[1:], F32),
            pltpu.VMEM((rows, width), F32),
            pltpu.VMEM((rows, width), F32),
            pltpu.VMEM((2, r, 4 * pr), F32),
            pltpu.VMEM((r, prior.shape[0]), F32),
            pltpu.VMEM((4, r, pr), F32),
            dma((8,)), dma((8,)), dma((8,)), dma((3,)),
            dma((4, 6, SUBS)), dma((4, 6, SUBS)),
            dma((4, 2, 2, SUBS)), dma((4, 4, SUBS)),
            dma((3, 3, SUBS)), dma((3, 4, SUBS)),
            dma((2, 4, SUBS)), dma((2, 4, SUBS)),
            dma((2, 4, SUBS)), dma((2, 4, SUBS)),
            dma((4, SUBS)), dma((4, SUBS)),
        ],
        compiler_params=pltpu.CompilerParams(collective_id=0, has_side_effects=True, vmem_limit_bytes=67043328),
    )(panel, prior.T, side, coupling, inverses)


def shards(nc, nr, panel, prior, right_side, coupling, inverses):
    q = nc // nr
    rows, width = coupling.shape
    r = prior.shape[1]
    pr = rows // nc
    dense = pr % 128 == 0
    lanes = 2 * r
    dma = pltpu.SemaphoreType.DMA
    hbm = pl.BlockSpec(memory_space=pl.ANY)
    vmem = pl.BlockSpec(memory_space=pltpu.VMEM)
    side = right_side.transpose(0, 2, 1)
    if nc == 8 and nr == 4 and dense:
        return paired_call(panel, prior, side, coupling, inverses).transpose(0, 2, 1)
    if not dense:
        side = side.reshape(2, r, nc, pr).transpose(0, 2, 1, 3)
    solved = pl.pallas_call(
        functools.partial(kernel, q, nr),
        out_shape=jax.ShapeDtypeStruct(side.shape, F32),
        in_specs=[hbm, vmem, hbm, hbm, hbm],
        out_specs=vmem,
        scratch_shapes=[
            pltpu.VMEM((q, nr, r, pr), F32),
            pltpu.VMEM((q, nr, r, pr), F32),
            pltpu.VMEM((4, q - 1, nr, r, pr), F32),
            pltpu.VMEM((4, nr - 1, r, pr), F32),
            pltpu.VMEM((4, r, pr), F32),
            pltpu.VMEM((3, nr, r, pr), F32),
            pltpu.VMEM((width, lanes), BF16),
            pltpu.VMEM((prior.shape[0], lanes), BF16),
            pltpu.VMEM(panel.shape[1:], F32),
            pltpu.VMEM((rows, width), F32),
            pltpu.VMEM((rows, width), F32),
            pltpu.VMEM((2, r, pr), F32),
            dma((nc,)), dma((nc,)), dma((nc,)), dma((2,)),
            dma((4, q - 1, nr, SUBS)), dma((4, q - 1, nr, SUBS)),
            dma((4, nr - 1, SUBS)), dma((4, nr - 1, SUBS)),
            dma((3, nr // 2, SUBS)), dma((3, nr, SUBS)), dma((3, nr, SUBS)),
            dma((2, nr - 1, SUBS)), dma((2, nr - 1, SUBS)),
            dma((2, q - 1, nr, SUBS)), dma((2, q - 1, nr, SUBS)),
        ],
        compiler_params=pltpu.CompilerParams(collective_id=0, has_side_effects=True, vmem_limit_bytes=67043328),
    )(panel, prior.T, side, coupling, inverses)
    if not dense:
        solved = solved.transpose(0, 2, 1, 3).reshape(2, r, rows)
    return solved.transpose(0, 2, 1)


def solution(mesh):
    in_specs = (
        P(None, "row", "col"),
        P("col", None),
        P(None, "row", None),
        P("row", "col"),
        P(None, "row", "col"),
    )
    out_specs = P(None, "row", None)
    body = functools.partial(shards, mesh.shape["col"], mesh.shape["row"])
    return jax.shard_map(body, mesh=mesh, in_specs=in_specs, out_specs=out_specs, check_vma=False)
```

```python
import functools
import jax
import jax.numpy as jnp
from jax import lax
from jax.experimental import pallas as pl
from jax.experimental.pallas import tpu as pltpu
from jax.sharding import PartitionSpec as P

F32, BF16 = jnp.float32, jnp.bfloat16
SUBS = 2
NT = (((1,), (1,)), ((), ()))


def kernel(q, nr, panel, prior, rs, coup, inv, out, part, part1, ra, rb, tv, xv, wv, w0, pbuf, buf0, buf1, rsv,
           psem, sem0, sem1, rsem, a_s, a_r, b_s, b_r, c1_s, x_r, c2_s, d_s, d_r, dy_s, dy_r):
    zn = nr
    nx = nr // 2
    r, pr = part.shape[2:]
    subs = range(SUBS)
    sub = [pl.ds(h * (r // SUBS), r // SUBS) for h in subs]
    col = lax.axis_index("col")
    i = lax.axis_index("row")
    z, y = lax.div(col, q), lax.rem(col, q)
    below = z <= i
    hub = z == i
    direct = lax.rem(i, 2) == lax.rem(z, 2)
    far = jnp.logical_and(direct, jnp.logical_not(hub))
    sibling = i + 1 - 2 * lax.rem(i, 2)

    def dev(zz, yy, ii):
        return {"col": zz * q + yy, "row": ii}

    def zfwd(k):
        return lax.rem(z + 1 + k, zn)

    def zback(k):
        return lax.rem(z + zn - 1 - k, zn)

    def yfwd(m):
        return lax.rem(y + 1 + m, q)

    def yback(m):
        return lax.rem(y + q - 1 - m, q)

    def remote(src, dst, ss, rr, to):
        return pltpu.make_async_remote_copy(
            src_ref=src, dst_ref=dst, send_sem=ss, recv_sem=rr, device_id=to, device_id_type=pl.DeviceIdType.MESH)

    def rows_of(m, k):
        return pl.ds(pl.multiple_of((yfwd(m) * zn + zfwd(k)) * pr, pr), pr)

    def load(src, dst, sem, m, k):
        rows = rows_of(m, k)
        return pltpu.make_async_copy(src.at[rows, :], dst.at[rows, :], sem.at[m * zn + k])

    def load_all(src, dst, sem):
        for m in range(q):
            pl.loop(0, zn)(lambda k, m=m: load(src, dst, sem, m, k).start())

    load_all(panel.at[0], pbuf, psem)

    def piece(ref, b, yy, zz):
        if len(ref.shape) == 4:
            return ref.at[b, yy * zn + zz]
        return ref.at[b, :, pl.ds(pl.multiple_of((yy * zn + zz) * pr, pr), pr)]

    rs_copies = [pltpu.make_async_copy(piece(rs, b, y, z), rsv.at[b], rsem.at[b]) for b in range(2)]
    for c in rs_copies:
        c.start()
    pl.when(below)(lambda: load_all(inv.at[0], buf0, sem0))

    barrier = pltpu.get_barrier_semaphore()
    for k in range(zn - 1):
        pl.semaphore_signal(barrier, inc=1, device_id=dev(zfwd(k), y, i), device_id_type=pl.DeviceIdType.MESH)
    for m in range(q - 1):
        pl.semaphore_signal(barrier, inc=1, device_id=dev(z, yfwd(m), i), device_id_type=pl.DeviceIdType.MESH)
    for n in range(nr - 1):
        pl.semaphore_signal(barrier, inc=1, device_id=dev(z, y, lax.rem(i + 1 + n, nr)), device_id_type=pl.DeviceIdType.MESH)

    @pl.when(far)
    def _():
        for k in range(zn):
            pl.semaphore_signal(barrier, inc=1, device_id=dev(k, y, z), device_id_type=pl.DeviceIdType.MESH)

    def split(x):
        high = x.astype(BF16).astype(F32)
        return jnp.concatenate([high, x - high], axis=0).T.astype(BF16)

    w0[...] = split(prior[...])
    for c in rs_copies:
        c.wait()
    pl.semaphore_wait(barrier, zn - 1 + q - 1 + nr - 1 + nx - 1)

    def product(buf, w, m, k):
        a = buf[rows_of(m, k), :]
        a1 = a.astype(BF16)
        a2 = (a - a1.astype(F32)).astype(BF16)
        p = jnp.dot(jnp.concatenate([a1, a2], axis=0), w[...], preferred_element_type=F32)
        s = (p[:pr] + p[pr:]).T
        return s[:r] + s[r:]

    def a_copy(ph, m, k, h):
        return remote(part.at[yfwd(m), zfwd(k), sub[h]], ra.at[ph, m, k, sub[h]], a_s.at[ph, m, k, h],
                      a_r.at[ph, m, k, h], dev(z, yfwd(m), i))

    def b_copy(ph, k, h):
        return remote(part.at[y, zfwd(k), sub[h]], rb.at[ph, k, sub[h]], b_s.at[ph, k, h], b_r.at[ph, k, h],
                      dev(zfwd(k), y, i))

    def guard(tri, cond, f):
        if tri:
            pl.when(cond)(f)
        else:
            f()

    def reduce(ph, src, buf, sem, w, tri, rhs, emit, add=False, after=None):
        def absorb(k, h):
            val = part[y, zfwd(k), sub[h]]
            for m in range(q - 1):
                a_copy(ph, m, k, h).wait_recv()
                val = val + ra[ph, m, k, sub[h]]
            part[y, zfwd(k), sub[h]] = val
            pl.when(k < zn - 1)(lambda: b_copy(ph, k, h).start())

        def compute():
            for m in range(q):
                @pl.loop(0, zn)
                def _(k):
                    load(src, buf, sem, m, k).wait()
                    val = product(buf, w, m, k)
                    if add:
                        val = val + part1[yfwd(m), zfwd(k)]
                    part[yfwd(m), zfwd(k)] = val
                    if after is not None:
                        load(after, buf, sem, m, k).start()
                    if m < q - 1:
                        a_copy(ph, m, k, 0).start()
                    else:
                        absorb(k, 0)

                if m < q - 1:
                    for h in subs[1:]:
                        pl.loop(0, zn)(lambda k, m=m, h=h: a_copy(ph, m, k, h).start())
            for h in subs[1:]:
                pl.loop(0, zn)(lambda k, h=h: absorb(k, h))

        guard(tri, below, compute)
        if tri:
            @pl.when(jnp.logical_not(below))
            def _():
                part[y, z] = jnp.zeros((r, pr), F32)
        for h in subs:
            for k in range(zn - 1):
                def take(k=k):
                    b_copy(ph, k, h).wait_recv()
                    part[y, z, sub[h]] = part[y, z, sub[h]] + rb[ph, k, sub[h]]

                guard(tri, zback(k) <= i, take)
            val = part[y, z, sub[h]]
            tv[ph, sub[h]] = val if rhs is None else rsv[rhs, sub[h]] - val
            emit(ph, h)

    def drain(ph, tri):
        def waits():
            for h in subs:
                for m in range(q - 1):
                    pl.loop(0, zn)(lambda k, m=m: a_copy(ph, m, k, h).wait_send())
                pl.loop(0, zn - 1)(lambda k: b_copy(ph, k, h).wait_send())

        guard(tri, below, waits)

    def up(ph, n, h):
        return remote(tv.at[ph, sub[h]], xv.at[ph, z, sub[h]], c1_s.at[ph, n, h], x_r.at[ph, z, h],
                      dev(i, y, lax.rem(i + 2 * n, nr)))

    def fwd(ph, s, h):
        there = xv.at[ph, s, sub[h]]
        return remote(there, there, c2_s.at[ph, s, h], x_r.at[ph, s, h], dev(z, y, sibling))

    def rise(ph, h):
        @pl.when(hub)
        def _():
            xv[ph, z, sub[h]] = tv[ph, sub[h]]

        for n in range(1, nx):
            up(ph, n, h).start()
        pl.when(jnp.logical_not(hub))(lambda: up(ph, 0, h).start())

    def spread(ph):
        for h in subs:
            @pl.loop(0, zn)
            def _(k):
                s = lax.rem(z + k, zn)
                pl.when(jnp.logical_not(jnp.logical_and(hub, s == z)))(lambda: fwd(ph, s, h).wait_recv())
                pl.when(direct)(lambda: fwd(ph, s, h).start())
                if h == SUBS - 1:
                    wv[pl.ds(pl.multiple_of(s * pr, pr), pr), :] = split(xv[ph, s])

    def spread_end(ph):
        for h in subs:
            for n in range(1, nx):
                up(ph, n, h).wait_send()
            pl.when(jnp.logical_not(hub))(lambda: up(ph, 0, h).wait_send())
            pl.when(direct)(lambda: pl.loop(0, zn)(lambda s: fwd(ph, s, h).wait_send()))

    def at_out(b, yy, zz, h):
        return piece(out, b, yy, zz).at[sub[h]]

    def dz_copy(b, ph, k, h, zz):
        return remote(tv.at[ph, sub[h]], at_out(b, y, zz, h), d_s.at[b, k, h], d_r.at[b, k, h], dev(zfwd(k), y, i))

    def dy_copy(b, m, slot, s, h, yy):
        return remote(at_out(b, y, s, h), at_out(b, yy, s, h), dy_s.at[b, m, slot, h], dy_r.at[b, m, slot, h],
                      dev(z, yfwd(m), i))

    def publish_z(b, ph, h):
        at_out(b, y, z, h)[...] = tv[ph, sub[h]]
        for k in range(zn - 1):
            dz_copy(b, ph, k, h, z).start()

    def publish_own(b, h):
        for m in range(q - 1):
            dy_copy(b, m, 0, z, h, y).start()

    def publish_y(b, ph, h):
        for k in range(zn - 1):
            dz_copy(b, ph, k, h, zback(k)).wait_recv()
            for m in range(q - 1):
                dy_copy(b, m, k + 1, zback(k), h, y).start()

    def publish_end(b, ph):
        for h in subs:
            for slot in range(zn):
                s = z if slot == 0 else zback(slot - 1)
                for m in range(q - 1):
                    dy_copy(b, m, slot, s, h, yback(m)).wait_recv()
                    dy_copy(b, m, slot, s, h, y).wait_send()
            for k in range(zn - 1):
                dz_copy(b, ph, k, h, z).wait_send()

    def second_carried():
        for m in range(q):
            @pl.loop(0, zn)
            def _(k):
                load(panel.at[1], pbuf, psem, m, k).wait()
                part1[yfwd(m), zfwd(k)] = product(pbuf, w0, m, k)

    def last(ph, h):
        publish_z(1, ph, h)
        publish_own(1, h)

    reduce(0, panel.at[0], pbuf, psem, w0, False, 0, rise, after=panel.at[1])
    second_carried()
    load_all(coup, buf1, sem1)
    spread(0)
    drain(0, False)
    reduce(1, inv.at[0], buf0, sem0, wv, True, None, rise, after=inv.at[1])
    spread(1)
    drain(1, True)
    publish_z(0, 1, 0)
    reduce(2, coup, buf1, sem1, wv, False, 1, rise, add=True)
    publish_own(0, 0)
    publish_y(0, 1, 0)
    spread(2)
    drain(2, False)
    for h in subs[1:]:
        publish_z(0, 1, h)
        publish_own(0, h)
    reduce(3, inv.at[1], buf0, sem0, wv, True, None, last)
    for h in subs[1:]:
        publish_y(0, 1, h)
    for h in subs:
        publish_y(1, 3, h)
    drain(3, True)
    for ph in range(3):
        spread_end(ph)
    publish_end(0, 1)
    publish_end(1, 3)


def paired(panel, prior, rs, coup, inv, out, part, part1, r1, r2, xv, wv, w0, pbuf, buf0, buf1, rsv, priv, lead,
           psem, sem0, sem1, rsem, s1_s, s1_r, s2_s, s2_r, s3_s, s3_r, o_s, o_r, f_s, f_r, l_s, l_r):
    zn = nr = 4
    kinds = 4
    r, pr = part.shape[2:]
    subs = range(SUBS)
    sub = [pl.ds(n * (r // SUBS), r // SUBS) for n in subs]
    low = [pl.ds(r + n * (r // SUBS), r // SUBS) for n in subs]
    col = lax.axis_index("col")
    i = lax.axis_index("row")
    z, y = lax.div(col, 2), lax.rem(col, 2)
    x, c = lax.div(i, 2), lax.rem(i, 2)
    across = lax.rem(i + 2, nr)
    sibling = i + 1 - 2 * c
    others = [across, lax.rem(sibling + 2, nr), sibling]
    hub = z == i
    below = z <= i
    below_across = z <= across

    def dev(zz, yy, ii):
        return {"col": zz * 2 + yy, "row": ii}

    def remote(src, dst, ss, rr, to):
        return pltpu.make_async_remote_copy(
            src_ref=src, dst_ref=dst, send_sem=ss, recv_sem=rr, device_id=to, device_id_type=pl.DeviceIdType.MESH)

    barrier = pltpu.get_barrier_semaphore()

    def greet(to):
        pl.semaphore_signal(barrier, inc=1, device_id=to, device_id_type=pl.DeviceIdType.MESH)

    greet(dev(z, 1 - y, i))
    greet(dev(z, 1 - y, across))
    for k in (2, 3, 1, 0):
        zz = lax.rem(z + k, zn)
        for n in range(0 if k else 1, nr):
            greet(dev(zz, y, lax.rem(i + n, nr)))
    greeted = 2 + zn * nr - 1

    def place(t):
        k, kind = lax.div(t, kinds), lax.rem(t, kinds)
        return k, kind, lax.rem(y + 1 - lax.div(kind, 2), 2), lax.rem(x + 1 - lax.rem(kind, 2), 2)

    def rows_of(t):
        k, _, h, xx = place(t)
        return pl.ds(pl.multiple_of((h * nr + 2 * xx + k) * pr, pr), pr)

    def load(src, dst, sem, t):
        rows = rows_of(t)
        return pltpu.make_async_copy(src.at[rows, :], dst.at[rows, :], sem.at[t])

    def used(t):
        kind = lax.rem(t, kinds)
        return jnp.logical_or(z < i, jnp.logical_and(hub, jnp.logical_or(y == 0, kind >= 2)))

    def guard(tri, cond, f):
        if tri:
            pl.when(cond)(f)
        else:
            f()

    def load_all(src, dst, sem, tri):
        @pl.loop(0, 2 * kinds)
        def _(t):
            guard(tri, used(t), lambda: load(src, dst, sem, t).start())

    known = pltpu.make_async_copy(prior, priv, rsem.at[2])
    known.start()
    load_all(panel.at[0], pbuf, psem, False)

    def side(b):
        lanes = pl.ds(pl.multiple_of(y * nr * pr, nr * pr), nr * pr)
        return pltpu.make_async_copy(rs.at[b, :, lanes], rsv.at[b], rsem.at[b])

    @pl.when(hub)
    def _():
        for b in range(2):
            side(b).start()

    def halves(v):
        high = v.astype(BF16)
        return high, (v - high.astype(F32)).astype(BF16)

    known.wait()
    w0[:r, :], w0[r:, :] = halves(priv[...])

    def product(buf, w, t):
        a1, a2 = halves(buf[rows_of(t), :])
        p = lax.dot_general(w[...], a1, NT, preferred_element_type=F32)
        p = p + lax.dot_general(w[...], a2, NT, preferred_element_type=F32)
        return p[:r] + p[r:]

    def s1(ph, t, n):
        k, kind, h, xx = place(t)
        slot = k * 3 + kind
        return remote(part.at[ph, t, sub[n]], r1.at[ph, slot, sub[n]], s1_s.at[ph, slot, n], s1_r.at[ph, slot, n],
                      dev(z, h, 2 * xx + c))

    def s1_start(ph, t):
        @pl.when(lax.rem(t, kinds) < 3)
        def _():
            for n in subs:
                s1(ph, t, n).start()

    def less_side(ref, b, t):
        k, kind, _, xx = place(t)

        @pl.when(jnp.logical_and(hub, kind >= 2))
        def _():
            lanes = pl.ds(pl.multiple_of((2 * xx + k) * pr, pr), pr)
            ref[...] = ref[...] - rsv[b, :, lanes]

    def s2(ph, k, own, n):
        src = part.at[ph, k * kinds + 3, sub[n]] if own else r1.at[ph, k * 3 + 2, sub[n]]
        return remote(src, r2.at[ph, z, sub[n]], s2_s.at[ph, k, int(own), n], s2_r.at[ph, z, n],
                      dev(i if own else across, y, 2 * x + k))

    def s2_here(k, own):
        return jnp.logical_and(z == (i if own else across), c == k)

    def gather(ph, k, n, tri, own):
        row = i if own else across
        slot = k * 3 + (1 if own else 0)
        val = part.at[ph, k * kinds + 3, sub[n]] if own else r1.at[ph, k * 3 + 2, sub[n]]

        def collect():
            if not own:
                s1(ph, k * kinds + 2, n).wait_recv()

            def add():
                s1(ph, slot - k * 3 + k * kinds, n).wait_recv()
                val[...] = val[...] + r1[ph, slot, sub[n]]

            guard(tri, jnp.logical_or(z < row, y == 1), add)
            here = s2_here(k, own)

            @pl.when(here)
            def _():
                r2[ph, z, sub[n]] = val[...]

            pl.when(jnp.logical_not(here))(lambda: s2(ph, k, own, n).start())

        guard(tri, z <= row, collect)

    def s3(ph, m, n):
        there = xv.at[ph, i, sub[n]]
        return remote(there, there, s3_s.at[ph, m, n], s3_r.at[ph, i, n], dev(z, y, others[m]))

    def s3_from(ph, m, n):
        there = xv.at[ph, others[m], sub[n]]
        return remote(there, there, s3_s.at[ph, m, n], s3_r.at[ph, others[m], n], dev(z, y, others[m]))

    def at_out(b, yy, q, n):
        return out.at[b, sub[n], pl.ds(pl.multiple_of((yy * nr + q) * pr, pr), pr)]

    def publish(b, ph, k, n):
        return remote(xv.at[ph, i, sub[n]], at_out(b, y, i, n), o_s.at[b, k, n], o_r.at[b, i, n],
                      dev(lax.rem(z + k, zn), y, z))

    def published(b, ph, q, n):
        return remote(xv.at[ph, i, sub[n]], at_out(b, y, q, n), o_s.at[b, 0, n], o_r.at[b, q, n], dev(i, y, q))

    def relay(k, n):
        return remote(xv.at[1, i, sub[n]], lead.at[z, sub[n]], l_s.at[k, n], l_r.at[z, n], dev(lax.rem(z + k, zn), y, i))

    def relayed(zz, n):
        return remote(lead.at[zz, sub[n]], lead.at[zz, sub[n]], l_s.at[0, n], l_r.at[zz, n], dev(zz, y, i))

    def deliver(j, n):
        return remote(lead.at[j, sub[n]], at_out(0, y, i, n), o_s.at[0, j, n], o_r.at[0, i, n], dev(z, y, j))

    def relay_all():
        lead[z] = xv[1, i]
        for n in subs:
            for k in (2, 1, 3):
                relay(k, n).start()

    def deliver_all():
        for n in subs:
            for j in range(nr):
                pl.when(z != j)(lambda j=j, n=n: relayed(j, n).wait_recv())
                pl.when(i != j)(lambda j=j, n=n: deliver(j, n).start())

                pl.when(i == j)(lambda j=j, n=n: keep(0, 1, n).start())

    def keep(b, ph, n):
        src = lead.at[i, sub[n]] if b == 0 else xv.at[ph, i, sub[n]]
        return pltpu.make_async_copy(src, at_out(b, y, i, n), o_r.at[b, i, n])

    def here(b, q):
        return i == q if b == 0 else jnp.logical_and(hub, i == q)

    def pass_on(b, q, n, yy):
        return remote(at_out(b, yy, q, n), at_out(b, yy, q, n), f_s.at[b, q, n], f_r.at[b, q, n], dev(z, 1 - y, i))

    def finish(ph, n, tri, sign, b):
        mine = lax.rem(z, 2) == c
        for zz in range(zn):
            def arrive(zz=zz):
                away = jnp.logical_not(jnp.logical_and(z == zz, mine))
                pl.when(away)(lambda: remote(
                    r2.at[ph, zz, sub[n]], r2.at[ph, zz, sub[n]], s2_s.at[ph, 0, 0, n], s2_r.at[ph, zz, n],
                    dev(zz, y, sibling)).wait_recv())
                val = r2[ph, zz, sub[n]]
                val = val if sign > 0 else -val
                xv[ph, i, sub[n]] = val if zz == 0 else xv[ph, i, sub[n]] + val

            guard(tri and zz > 0, zz <= z, arrive)
        if ph < 3:
            for m in range(3):
                s3(ph, m, n).start()
        if b == 1:
            for k in (2, 3, 1):
                publish(b, ph, k, n).start()
            pl.when(jnp.logical_not(hub))(lambda: publish(b, ph, 0, n).start())

            pl.when(hub)(lambda: keep(b, ph, n).start())

    def reduce(ph, tri, sign, b=None, between=None):
        for n in subs:
            pl.when(c == 0)(lambda n=n: finish(ph, n, tri, sign, b))
            gather(ph, 1, n, tri, True)
            gather(ph, 1, n, tri, False)
        if between is not None:
            between()
        for n in subs:
            pl.when(c == 1)(lambda n=n: finish(ph, n, tri, sign, b))

    def drain(ph, tri):
        for k in range(2):
            for n in subs:
                for kind in range(3):
                    t = k * kinds + kind
                    guard(tri, used(t), lambda t=t, n=n: s1(ph, t, n).wait_send())
                for own, cond in ((True, below), (False, below_across)):
                    live = jnp.logical_not(s2_here(k, own))
                    if tri:
                        live = jnp.logical_and(live, cond)
                    pl.when(live)(lambda k=k, n=n, own=own: s2(ph, k, own, n).wait_send())

    def spread(ph):
        def put(q, n):
            lanes = pl.ds(pl.multiple_of(q * pr, pr), pr)
            wv[sub[n], lanes], wv[low[n], lanes] = halves(xv[ph, q, sub[n]])

        for n in subs:
            put(i, n)
        for m in (2, 0, 1):
            for n in subs:
                s3_from(ph, m, n).wait_recv()
                put(others[m], n)

    def spread_end(ph):
        for m in range(3):
            for n in subs:
                s3(ph, m, n).wait_send()

    def hand_over(b, ph):
        for q in (0, 2, 1, 3):
            for n in subs:
                pl.when(jnp.logical_not(here(b, q)))(lambda q=q, n=n: published(b, ph, q, n).wait_recv())
                pl.when(here(b, q))(lambda n=n: keep(b, ph, n).wait())
                pass_on(b, q, n, y).start()

    def sent_end(b, ph):
        for n in subs:
            if b == 1:
                for k in range(1, zn):
                    publish(b, ph, k, n).wait_send()
                pl.when(jnp.logical_not(hub))(lambda n=n: publish(b, ph, 0, n).wait_send())
            else:
                for k in range(1, zn):
                    relay(k, n).wait_send()
                for j in range(nr):
                    pl.when(i != j)(lambda j=j, n=n: deliver(j, n).wait_send())

    def hand_over_end(b, ph):
        for n in subs:
            for q in range(nr):
                pass_on(b, q, n, y).wait_send()
                pass_on(b, q, n, 1 - y).wait_recv()

    def multiply(ph, src, buf, sem, w, tri, after=None, more=False):
        @pl.loop(0, 2 * kinds)
        def _(t):
            def piece():
                load(src, buf, sem, t).wait()
                val = product(buf, w, t)
                if more:
                    val = val + part1[t]
                part[ph, t] = val
                s1_start(ph, t)
                if after is not None:
                    load(after, buf, sem, t).start()

            guard(tri, used(t), piece)
            for n in subs:
                pl.when(t == kinds + 1 + n)(lambda n=n: gather(ph, 0, n, tri, True))
                pl.when(t == kinds + 1 + n)(lambda n=n: gather(ph, 0, n, tri, False))

    @pl.loop(0, 2 * kinds)
    def _(t):
        load(panel.at[0], pbuf, psem, t).wait()
        part[0, t] = product(pbuf, w0, t)
        load(panel.at[1], pbuf, psem, t).start()

    @pl.when(hub)
    def _():
        for b in range(2):
            side(b).wait()
        pl.loop(0, 2 * kinds)(lambda t: less_side(part.at[0, t], 0, t))

    pl.semaphore_wait(barrier, greeted)
    for k in range(2):
        for n in subs:
            for kind in range(3):
                s1(0, k * kinds + kind, n).start()
    load_all(inv.at[0], buf0, sem0, True)

    @pl.loop(0, 2 * kinds)
    def _(t):
        load(panel.at[1], pbuf, psem, t).wait()
        part1[t] = product(pbuf, w0, t)
        less_side(part1.at[t], 1, t)

    load_all(coup, buf1, sem1, False)
    for n in subs:
        for own in (True, False):
            gather(0, 0, n, False, own)
    reduce(0, False, -1)
    spread(0)
    multiply(1, inv.at[0], buf0, sem0, wv, True, after=inv.at[1])
    reduce(1, True, 1, 0)
    relay_all()
    spread(1)
    multiply(2, coup, buf1, sem1, wv, False, more=True)
    reduce(2, False, -1, between=deliver_all)
    spread(2)
    multiply(3, inv.at[1], buf0, sem0, wv, True)
    reduce(3, True, 1, 1, between=lambda: hand_over(0, 1))
    for ph in range(4):
        drain(ph, ph % 2 == 1)
    for ph in range(3):
        spread_end(ph)
    sent_end(0, 1)
    hand_over(1, 3)
    hand_over_end(0, 1)
    sent_end(1, 3)
    hand_over_end(1, 3)


def paired_call(panel, prior, side, coupling, inverses):
    rows, width = coupling.shape
    r = prior.shape[1]
    pr = rows // 8
    dma = pltpu.SemaphoreType.DMA
    hbm = pl.BlockSpec(memory_space=pl.ANY)
    return pl.pallas_call(
        paired,
        out_shape=jax.ShapeDtypeStruct(side.shape, F32),
        in_specs=[hbm, hbm, hbm, hbm, hbm],
        out_specs=hbm,
        scratch_shapes=[
            pltpu.VMEM((4, 8, r, pr), F32),
            pltpu.VMEM((8, r, pr), F32),
            pltpu.VMEM((4, 6, r, pr), F32),
            pltpu.VMEM((4, 4, r, pr), F32),
            pltpu.VMEM((4, 4, r, pr), F32),
            pltpu.VMEM((2 * r, width), BF16),
            pltpu.VMEM((2 * r, prior.shape[0]), BF16),
            pltpu.VMEM(panel.shape[1:], F32),
            pltpu.VMEM((rows, width), F32),
            pltpu.VMEM((rows, width), F32),
            pltpu.VMEM((2, r, 4 * pr), F32),
            pltpu.VMEM((r, prior.shape[0]), F32),
            pltpu.VMEM((4, r, pr), F32),
            dma((8,)), dma((8,)), dma((8,)), dma((3,)),
            dma((4, 6, SUBS)), dma((4, 6, SUBS)),
            dma((4, 2, 2, SUBS)), dma((4, 4, SUBS)),
            dma((3, 3, SUBS)), dma((3, 4, SUBS)),
            dma((2, 4, SUBS)), dma((2, 4, SUBS)),
            dma((2, 4, SUBS)), dma((2, 4, SUBS)),
            dma((4, SUBS)), dma((4, SUBS)),
        ],
        compiler_params=pltpu.CompilerParams(collective_id=0, has_side_effects=True, vmem_limit_bytes=67043328),
    )(panel, prior.T, side, coupling, inverses)


def shards(nc, nr, panel, prior, right_side, coupling, inverses):
    q = nc // nr
    rows, width = coupling.shape
    r = prior.shape[1]
    pr = rows // nc
    dense = pr % 128 == 0
    lanes = 2 * r
    dma = pltpu.SemaphoreType.DMA
    hbm = pl.BlockSpec(memory_space=pl.ANY)
    vmem = pl.BlockSpec(memory_space=pltpu.VMEM)
    side = right_side.transpose(0, 2, 1)
    if nc == 8 and nr == 4 and dense:
        return paired_call(panel, prior, side, coupling, inverses).transpose(0, 2, 1)
    if not dense:
        side = side.reshape(2, r, nc, pr).transpose(0, 2, 1, 3)
    solved = pl.pallas_call(
        functools.partial(kernel, q, nr),
        out_shape=jax.ShapeDtypeStruct(side.shape, F32),
        in_specs=[hbm, vmem, hbm, hbm, hbm],
        out_specs=vmem,
        scratch_shapes=[
            pltpu.VMEM((q, nr, r, pr), F32),
            pltpu.VMEM((q, nr, r, pr), F32),
            pltpu.VMEM((4, q - 1, nr, r, pr), F32),
            pltpu.VMEM((4, nr - 1, r, pr), F32),
            pltpu.VMEM((4, r, pr), F32),
            pltpu.VMEM((3, nr, r, pr), F32),
            pltpu.VMEM((width, lanes), BF16),
            pltpu.VMEM((prior.shape[0], lanes), BF16),
            pltpu.VMEM(panel.shape[1:], F32),
            pltpu.VMEM((rows, width), F32),
            pltpu.VMEM((rows, width), F32),
            pltpu.VMEM((2, r, pr), F32),
            dma((nc,)), dma((nc,)), dma((nc,)), dma((2,)),
            dma((4, q - 1, nr, SUBS)), dma((4, q - 1, nr, SUBS)),
            dma((4, nr - 1, SUBS)), dma((4, nr - 1, SUBS)),
            dma((3, nr // 2, SUBS)), dma((3, nr, SUBS)), dma((3, nr, SUBS)),
            dma((2, nr - 1, SUBS)), dma((2, nr - 1, SUBS)),
            dma((2, q - 1, nr, SUBS)), dma((2, q - 1, nr, SUBS)),
        ],
        compiler_params=pltpu.CompilerParams(collective_id=0, has_side_effects=True, vmem_limit_bytes=67043328),
    )(panel, prior.T, side, coupling, inverses)
    if not dense:
        solved = solved.transpose(0, 2, 1, 3).reshape(2, r, rows)
    return solved.transpose(0, 2, 1)


def solution(mesh):
    in_specs = (
        P(None, "row", "col"),
        P("col", None),
        P(None, "row", None),
        P("row", "col"),
        P(None, "row", "col"),
    )
    out_specs = P(None, "row", None)
    body = functools.partial(shards, mesh.shape["col"], mesh.shape["row"])
    return jax.shard_map(body, mesh=mesh, in_specs=in_specs, out_specs=out_specs, check_vma=False)
```

```python
import functools
import jax
import jax.numpy as jnp
from jax import lax
from jax.experimental import pallas as pl
from jax.experimental.pallas import tpu as pltpu
from jax.sharding import PartitionSpec as P

F32, BF16 = jnp.float32, jnp.bfloat16
SUBS = 2
NT = (((1,), (1,)), ((), ()))


def kernel(q, nr, panel, prior, rs, coup, inv, out, part, part1, ra, rb, tv, xv, wv, w0, pbuf, buf0, buf1, rsv,
           psem, sem0, sem1, rsem, a_s, a_r, b_s, b_r, c1_s, x_r, c2_s, d_s, d_r, dy_s, dy_r):
    zn = nr
    nx = nr // 2
    r, pr = part.shape[2:]
    subs = range(SUBS)
    sub = [pl.ds(h * (r // SUBS), r // SUBS) for h in subs]
    col = lax.axis_index("col")
    i = lax.axis_index("row")
    z, y = lax.div(col, q), lax.rem(col, q)
    below = z <= i
    hub = z == i
    direct = lax.rem(i, 2) == lax.rem(z, 2)
    far = jnp.logical_and(direct, jnp.logical_not(hub))
    sibling = i + 1 - 2 * lax.rem(i, 2)

    def dev(zz, yy, ii):
        return {"col": zz * q + yy, "row": ii}

    def zfwd(k):
        return lax.rem(z + 1 + k, zn)

    def zback(k):
        return lax.rem(z + zn - 1 - k, zn)

    def yfwd(m):
        return lax.rem(y + 1 + m, q)

    def yback(m):
        return lax.rem(y + q - 1 - m, q)

    def remote(src, dst, ss, rr, to):
        return pltpu.make_async_remote_copy(
            src_ref=src, dst_ref=dst, send_sem=ss, recv_sem=rr, device_id=to, device_id_type=pl.DeviceIdType.MESH)

    def rows_of(m, k):
        return pl.ds(pl.multiple_of((yfwd(m) * zn + zfwd(k)) * pr, pr), pr)

    def load(src, dst, sem, m, k):
        rows = rows_of(m, k)
        return pltpu.make_async_copy(src.at[rows, :], dst.at[rows, :], sem.at[m * zn + k])

    def load_all(src, dst, sem):
        for m in range(q):
            pl.loop(0, zn)(lambda k, m=m: load(src, dst, sem, m, k).start())

    load_all(panel.at[0], pbuf, psem)

    def piece(ref, b, yy, zz):
        if len(ref.shape) == 4:
            return ref.at[b, yy * zn + zz]
        return ref.at[b, :, pl.ds(pl.multiple_of((yy * zn + zz) * pr, pr), pr)]

    rs_copies = [pltpu.make_async_copy(piece(rs, b, y, z), rsv.at[b], rsem.at[b]) for b in range(2)]
    for c in rs_copies:
        c.start()
    pl.when(below)(lambda: load_all(inv.at[0], buf0, sem0))

    barrier = pltpu.get_barrier_semaphore()
    for k in range(zn - 1):
        pl.semaphore_signal(barrier, inc=1, device_id=dev(zfwd(k), y, i), device_id_type=pl.DeviceIdType.MESH)
    for m in range(q - 1):
        pl.semaphore_signal(barrier, inc=1, device_id=dev(z, yfwd(m), i), device_id_type=pl.DeviceIdType.MESH)
    for n in range(nr - 1):
        pl.semaphore_signal(barrier, inc=1, device_id=dev(z, y, lax.rem(i + 1 + n, nr)), device_id_type=pl.DeviceIdType.MESH)

    @pl.when(far)
    def _():
        for k in range(zn):
            pl.semaphore_signal(barrier, inc=1, device_id=dev(k, y, z), device_id_type=pl.DeviceIdType.MESH)

    def split(x):
        high = x.astype(BF16).astype(F32)
        return jnp.concatenate([high, x - high], axis=0).T.astype(BF16)

    w0[...] = split(prior[...])
    for c in rs_copies:
        c.wait()
    pl.semaphore_wait(barrier, zn - 1 + q - 1 + nr - 1 + nx - 1)

    def product(buf, w, m, k):
        a = buf[rows_of(m, k), :]
        a1 = a.astype(BF16)
        a2 = (a - a1.astype(F32)).astype(BF16)
        p = jnp.dot(jnp.concatenate([a1, a2], axis=0), w[...], preferred_element_type=F32)
        s = (p[:pr] + p[pr:]).T
        return s[:r] + s[r:]

    def a_copy(ph, m, k, h):
        return remote(part.at[yfwd(m), zfwd(k), sub[h]], ra.at[ph, m, k, sub[h]], a_s.at[ph, m, k, h],
                      a_r.at[ph, m, k, h], dev(z, yfwd(m), i))

    def b_copy(ph, k, h):
        return remote(part.at[y, zfwd(k), sub[h]], rb.at[ph, k, sub[h]], b_s.at[ph, k, h], b_r.at[ph, k, h],
                      dev(zfwd(k), y, i))

    def guard(tri, cond, f):
        if tri:
            pl.when(cond)(f)
        else:
            f()

    def reduce(ph, src, buf, sem, w, tri, rhs, emit, add=False, after=None):
        def absorb(k, h):
            val = part[y, zfwd(k), sub[h]]
            for m in range(q - 1):
                a_copy(ph, m, k, h).wait_recv()
                val = val + ra[ph, m, k, sub[h]]
            part[y, zfwd(k), sub[h]] = val
            pl.when(k < zn - 1)(lambda: b_copy(ph, k, h).start())

        def compute():
            for m in range(q):
                @pl.loop(0, zn)
                def _(k):
                    load(src, buf, sem, m, k).wait()
                    val = product(buf, w, m, k)
                    if add:
                        val = val + part1[yfwd(m), zfwd(k)]
                    part[yfwd(m), zfwd(k)] = val
                    if after is not None:
                        load(after, buf, sem, m, k).start()
                    if m < q - 1:
                        a_copy(ph, m, k, 0).start()
                    else:
                        absorb(k, 0)

                if m < q - 1:
                    for h in subs[1:]:
                        pl.loop(0, zn)(lambda k, m=m, h=h: a_copy(ph, m, k, h).start())
            for h in subs[1:]:
                pl.loop(0, zn)(lambda k, h=h: absorb(k, h))

        guard(tri, below, compute)
        if tri:
            @pl.when(jnp.logical_not(below))
            def _():
                part[y, z] = jnp.zeros((r, pr), F32)
        for h in subs:
            for k in range(zn - 1):
                def take(k=k):
                    b_copy(ph, k, h).wait_recv()
                    part[y, z, sub[h]] = part[y, z, sub[h]] + rb[ph, k, sub[h]]

                guard(tri, zback(k) <= i, take)
            val = part[y, z, sub[h]]
            tv[ph, sub[h]] = val if rhs is None else rsv[rhs, sub[h]] - val
            emit(ph, h)

    def drain(ph, tri):
        def waits():
            for h in subs:
                for m in range(q - 1):
                    pl.loop(0, zn)(lambda k, m=m: a_copy(ph, m, k, h).wait_send())
                pl.loop(0, zn - 1)(lambda k: b_copy(ph, k, h).wait_send())

        guard(tri, below, waits)

    def up(ph, n, h):
        return remote(tv.at[ph, sub[h]], xv.at[ph, z, sub[h]], c1_s.at[ph, n, h], x_r.at[ph, z, h],
                      dev(i, y, lax.rem(i + 2 * n, nr)))

    def fwd(ph, s, h):
        there = xv.at[ph, s, sub[h]]
        return remote(there, there, c2_s.at[ph, s, h], x_r.at[ph, s, h], dev(z, y, sibling))

    def rise(ph, h):
        @pl.when(hub)
        def _():
            xv[ph, z, sub[h]] = tv[ph, sub[h]]

        for n in range(1, nx):
            up(ph, n, h).start()
        pl.when(jnp.logical_not(hub))(lambda: up(ph, 0, h).start())

    def spread(ph):
        for h in subs:
            @pl.loop(0, zn)
            def _(k):
                s = lax.rem(z + k, zn)
                pl.when(jnp.logical_not(jnp.logical_and(hub, s == z)))(lambda: fwd(ph, s, h).wait_recv())
                pl.when(direct)(lambda: fwd(ph, s, h).start())
                if h == SUBS - 1:
                    wv[pl.ds(pl.multiple_of(s * pr, pr), pr), :] = split(xv[ph, s])

    def spread_end(ph):
        for h in subs:
            for n in range(1, nx):
                up(ph, n, h).wait_send()
            pl.when(jnp.logical_not(hub))(lambda: up(ph, 0, h).wait_send())
            pl.when(direct)(lambda: pl.loop(0, zn)(lambda s: fwd(ph, s, h).wait_send()))

    def at_out(b, yy, zz, h):
        return piece(out, b, yy, zz).at[sub[h]]

    def dz_copy(b, ph, k, h, zz):
        return remote(tv.at[ph, sub[h]], at_out(b, y, zz, h), d_s.at[b, k, h], d_r.at[b, k, h], dev(zfwd(k), y, i))

    def dy_copy(b, m, slot, s, h, yy):
        return remote(at_out(b, y, s, h), at_out(b, yy, s, h), dy_s.at[b, m, slot, h], dy_r.at[b, m, slot, h],
                      dev(z, yfwd(m), i))

    def publish_z(b, ph, h):
        at_out(b, y, z, h)[...] = tv[ph, sub[h]]
        for k in range(zn - 1):
            dz_copy(b, ph, k, h, z).start()

    def publish_own(b, h):
        for m in range(q - 1):
            dy_copy(b, m, 0, z, h, y).start()

    def publish_y(b, ph, h):
        for k in range(zn - 1):
            dz_copy(b, ph, k, h, zback(k)).wait_recv()
            for m in range(q - 1):
                dy_copy(b, m, k + 1, zback(k), h, y).start()

    def publish_end(b, ph):
        for h in subs:
            for slot in range(zn):
                s = z if slot == 0 else zback(slot - 1)
                for m in range(q - 1):
                    dy_copy(b, m, slot, s, h, yback(m)).wait_recv()
                    dy_copy(b, m, slot, s, h, y).wait_send()
            for k in range(zn - 1):
                dz_copy(b, ph, k, h, z).wait_send()

    def second_carried():
        for m in range(q):
            @pl.loop(0, zn)
            def _(k):
                load(panel.at[1], pbuf, psem, m, k).wait()
                part1[yfwd(m), zfwd(k)] = product(pbuf, w0, m, k)

    def last(ph, h):
        publish_z(1, ph, h)
        publish_own(1, h)

    reduce(0, panel.at[0], pbuf, psem, w0, False, 0, rise, after=panel.at[1])
    second_carried()
    load_all(coup, buf1, sem1)
    spread(0)
    drain(0, False)
    reduce(1, inv.at[0], buf0, sem0, wv, True, None, rise, after=inv.at[1])
    spread(1)
    drain(1, True)
    publish_z(0, 1, 0)
    reduce(2, coup, buf1, sem1, wv, False, 1, rise, add=True)
    publish_own(0, 0)
    publish_y(0, 1, 0)
    spread(2)
    drain(2, False)
    for h in subs[1:]:
        publish_z(0, 1, h)
        publish_own(0, h)
    reduce(3, inv.at[1], buf0, sem0, wv, True, None, last)
    for h in subs[1:]:
        publish_y(0, 1, h)
    for h in subs:
        publish_y(1, 3, h)
    drain(3, True)
    for ph in range(3):
        spread_end(ph)
    publish_end(0, 1)
    publish_end(1, 3)


def paired(panel, prior, rs, coup, inv, out, part, part1, r1, r2, xv, wv, w0, pbuf, buf0, buf1, rsv, priv, lead,
           psem, sem0, sem1, rsem, s1_s, s1_r, s2_s, s2_r, s3_s, s3_r, o_s, o_r, f_s, f_r, l_s, l_r):
    zn = nr = 4
    kinds = 4
    r, pr = part.shape[2:]
    subs = range(SUBS)
    sub = [pl.ds(n * (r // SUBS), r // SUBS) for n in subs]
    low = [pl.ds(r + n * (r // SUBS), r // SUBS) for n in subs]
    col = lax.axis_index("col")
    i = lax.axis_index("row")
    z, y = lax.div(col, 2), lax.rem(col, 2)
    x, c = lax.div(i, 2), lax.rem(i, 2)
    across = lax.rem(i + 2, nr)
    sibling = i + 1 - 2 * c
    others = [across, lax.rem(sibling + 2, nr), sibling]
    hub = z == i
    below = z <= i
    below_across = z <= across

    def dev(zz, yy, ii):
        return {"col": zz * 2 + yy, "row": ii}

    def remote(src, dst, ss, rr, to):
        return pltpu.make_async_remote_copy(
            src_ref=src, dst_ref=dst, send_sem=ss, recv_sem=rr, device_id=to, device_id_type=pl.DeviceIdType.MESH)

    barrier = pltpu.get_barrier_semaphore()

    def greet(to):
        pl.semaphore_signal(barrier, inc=1, device_id=to, device_id_type=pl.DeviceIdType.MESH)

    greet(dev(z, 1 - y, i))
    greet(dev(z, 1 - y, across))
    for k in (2, 3, 1, 0):
        zz = lax.rem(z + k, zn)
        for n in range(0 if k else 1, nr):
            greet(dev(zz, y, lax.rem(i + n, nr)))
    greeted = 2 + zn * nr - 1

    def place(t):
        k, kind = lax.div(t, kinds), lax.rem(t, kinds)
        return k, kind, lax.rem(y + 1 - lax.div(kind, 2), 2), lax.rem(x + 1 - lax.rem(kind, 2), 2)

    def rows_of(t):
        k, _, h, xx = place(t)
        return pl.ds(pl.multiple_of((h * nr + 2 * xx + k) * pr, pr), pr)

    def load(src, dst, sem, t):
        rows = rows_of(t)
        return pltpu.make_async_copy(src.at[rows, :], dst.at[rows, :], sem.at[t])

    def used(t):
        kind = lax.rem(t, kinds)
        return jnp.logical_or(z < i, jnp.logical_and(hub, jnp.logical_or(y == 0, kind >= 2)))

    def guard(tri, cond, f):
        if tri:
            pl.when(cond)(f)
        else:
            f()

    def load_all(src, dst, sem, tri):
        @pl.loop(0, 2 * kinds)
        def _(t):
            guard(tri, used(t), lambda: load(src, dst, sem, t).start())

    known = pltpu.make_async_copy(prior, priv, rsem.at[2])
    known.start()
    load_all(panel.at[0], pbuf, psem, False)

    def side(b):
        lanes = pl.ds(pl.multiple_of(y * nr * pr, nr * pr), nr * pr)
        return pltpu.make_async_copy(rs.at[b, :, lanes], rsv.at[b], rsem.at[b])

    @pl.when(hub)
    def _():
        for b in range(2):
            side(b).start()

    def halves(v):
        high = v.astype(BF16)
        return high, (v - high.astype(F32)).astype(BF16)

    known.wait()
    w0[:r, :], w0[r:, :] = halves(priv[...])

    def product(buf, w, t):
        a1, a2 = halves(buf[rows_of(t), :])
        p = lax.dot_general(w[...], a1, NT, preferred_element_type=F32)
        p = p + lax.dot_general(w[...], a2, NT, preferred_element_type=F32)
        return p[:r] + p[r:]

    def s1(ph, t, n):
        k, kind, h, xx = place(t)
        slot = k * 3 + kind
        return remote(part.at[ph, t, sub[n]], r1.at[ph, slot, sub[n]], s1_s.at[ph, slot, n], s1_r.at[ph, slot, n],
                      dev(z, h, 2 * xx + c))

    def s1_start(ph, t):
        @pl.when(lax.rem(t, kinds) < 3)
        def _():
            for n in subs:
                s1(ph, t, n).start()

    def less_side(ref, b, t):
        k, kind, _, xx = place(t)

        @pl.when(jnp.logical_and(hub, kind >= 2))
        def _():
            lanes = pl.ds(pl.multiple_of((2 * xx + k) * pr, pr), pr)
            ref[...] = ref[...] - rsv[b, :, lanes]

    def s2(ph, k, own, n):
        src = part.at[ph, k * kinds + 3, sub[n]] if own else r1.at[ph, k * 3 + 2, sub[n]]
        return remote(src, r2.at[ph, z, sub[n]], s2_s.at[ph, k, int(own), n], s2_r.at[ph, z, n],
                      dev(i if own else across, y, 2 * x + k))

    def s2_here(k, own):
        return jnp.logical_and(z == (i if own else across), c == k)

    def gather(ph, k, n, tri, own):
        row = i if own else across
        slot = k * 3 + (1 if own else 0)
        val = part.at[ph, k * kinds + 3, sub[n]] if own else r1.at[ph, k * 3 + 2, sub[n]]

        def collect():
            if not own:
                s1(ph, k * kinds + 2, n).wait_recv()

            def add():
                s1(ph, slot - k * 3 + k * kinds, n).wait_recv()
                val[...] = val[...] + r1[ph, slot, sub[n]]

            guard(tri, jnp.logical_or(z < row, y == 1), add)
            here = s2_here(k, own)

            @pl.when(here)
            def _():
                r2[ph, z, sub[n]] = val[...]

            pl.when(jnp.logical_not(here))(lambda: s2(ph, k, own, n).start())

        guard(tri, z <= row, collect)

    def s3(ph, m, n):
        there = xv.at[ph, i, sub[n]]
        return remote(there, there, s3_s.at[ph, m, n], s3_r.at[ph, i, n], dev(z, y, others[m]))

    def s3_from(ph, m, n):
        there = xv.at[ph, others[m], sub[n]]
        return remote(there, there, s3_s.at[ph, m, n], s3_r.at[ph, others[m], n], dev(z, y, others[m]))

    def at_out(b, yy, q, n):
        return out.at[b, sub[n], pl.ds(pl.multiple_of((yy * nr + q) * pr, pr), pr)]

    def publish(b, ph, k, n):
        return remote(xv.at[ph, i, sub[n]], at_out(b, y, i, n), o_s.at[b, k, n], o_r.at[b, i, n],
                      dev(lax.rem(z + k, zn), y, z))

    def published(b, ph, q, n):
        return remote(xv.at[ph, i, sub[n]], at_out(b, y, q, n), o_s.at[b, 0, n], o_r.at[b, q, n], dev(i, y, q))

    def relay(k, n):
        return remote(xv.at[1, i, sub[n]], lead.at[z, sub[n]], l_s.at[k, n], l_r.at[z, n], dev(lax.rem(z + k, zn), y, i))

    def relayed(zz, n):
        return remote(lead.at[zz, sub[n]], lead.at[zz, sub[n]], l_s.at[0, n], l_r.at[zz, n], dev(zz, y, i))

    def deliver(j, n):
        return remote(lead.at[j, sub[n]], at_out(0, y, i, n), o_s.at[0, j, n], o_r.at[0, i, n], dev(z, y, j))

    def relay_all():
        lead[z] = xv[1, i]
        for n in subs:
            for k in (2, 1, 3):
                relay(k, n).start()

    def deliver_all():
        for n in subs:
            for j in range(nr):
                pl.when(z != j)(lambda j=j, n=n: relayed(j, n).wait_recv())
                pl.when(i != j)(lambda j=j, n=n: deliver(j, n).start())

                pl.when(i == j)(lambda j=j, n=n: keep(0, 1, n).start())

    def keep(b, ph, n):
        src = lead.at[i, sub[n]] if b == 0 else xv.at[ph, i, sub[n]]
        return pltpu.make_async_copy(src, at_out(b, y, i, n), o_r.at[b, i, n])

    def here(b, q):
        return i == q if b == 0 else jnp.logical_and(hub, i == q)

    def pass_on(b, q, n, yy):
        return remote(at_out(b, yy, q, n), at_out(b, yy, q, n), f_s.at[b, q, n], f_r.at[b, q, n], dev(z, 1 - y, i))

    def finish(ph, n, tri, sign, b):
        mine = lax.rem(z, 2) == c
        for zz in range(zn):
            def arrive(zz=zz):
                away = jnp.logical_not(jnp.logical_and(z == zz, mine))
                pl.when(away)(lambda: remote(
                    r2.at[ph, zz, sub[n]], r2.at[ph, zz, sub[n]], s2_s.at[ph, 0, 0, n], s2_r.at[ph, zz, n],
                    dev(zz, y, sibling)).wait_recv())
                val = r2[ph, zz, sub[n]]
                val = val if sign > 0 else -val
                xv[ph, i, sub[n]] = val if zz == 0 else xv[ph, i, sub[n]] + val

            guard(tri and zz > 0, zz <= z, arrive)
        if ph < 3:
            for m in range(3):
                s3(ph, m, n).start()
        if b == 1:
            for k in (2, 3, 1):
                publish(b, ph, k, n).start()
            pl.when(jnp.logical_not(hub))(lambda: publish(b, ph, 0, n).start())

            pl.when(hub)(lambda: keep(b, ph, n).start())

    def reduce(ph, tri, sign, b=None, between=None):
        for n in subs:
            gather(ph, 1, n, tri, True)
            gather(ph, 1, n, tri, False)
            pl.when(c == 0)(lambda n=n: finish(ph, n, tri, sign, b))
        if between is not None:
            between()
        for n in subs:
            pl.when(c == 1)(lambda n=n: finish(ph, n, tri, sign, b))

    def drain(ph, tri):
        for k in range(2):
            for n in subs:
                for kind in range(3):
                    t = k * kinds + kind
                    guard(tri, used(t), lambda t=t, n=n: s1(ph, t, n).wait_send())
                for own, cond in ((True, below), (False, below_across)):
                    live = jnp.logical_not(s2_here(k, own))
                    if tri:
                        live = jnp.logical_and(live, cond)
                    pl.when(live)(lambda k=k, n=n, own=own: s2(ph, k, own, n).wait_send())

    def spread(ph):
        def put(q, n):
            lanes = pl.ds(pl.multiple_of(q * pr, pr), pr)
            wv[sub[n], lanes], wv[low[n], lanes] = halves(xv[ph, q, sub[n]])

        for n in subs:
            put(i, n)
        for m in (2, 0, 1):
            for n in subs:
                s3_from(ph, m, n).wait_recv()
                put(others[m], n)

    def spread_end(ph):
        for m in range(3):
            for n in subs:
                s3(ph, m, n).wait_send()

    def hand_over(b, ph):
        for q in (0, 2, 1, 3):
            for n in subs:
                pl.when(jnp.logical_not(here(b, q)))(lambda q=q, n=n: published(b, ph, q, n).wait_recv())
                pl.when(here(b, q))(lambda n=n: keep(b, ph, n).wait())
                pass_on(b, q, n, y).start()

    def sent_end(b, ph):
        for n in subs:
            if b == 1:
                for k in range(1, zn):
                    publish(b, ph, k, n).wait_send()
                pl.when(jnp.logical_not(hub))(lambda n=n: publish(b, ph, 0, n).wait_send())
            else:
                for k in range(1, zn):
                    relay(k, n).wait_send()
                for j in range(nr):
                    pl.when(i != j)(lambda j=j, n=n: deliver(j, n).wait_send())

    def hand_over_end(b, ph):
        for n in subs:
            for q in range(nr):
                pass_on(b, q, n, y).wait_send()
                pass_on(b, q, n, 1 - y).wait_recv()

    def multiply(ph, src, buf, sem, w, tri, after=None, more=False):
        @pl.loop(0, 2 * kinds)
        def _(t):
            def piece():
                load(src, buf, sem, t).wait()
                val = product(buf, w, t)
                if more:
                    val = val + part1[t]
                part[ph, t] = val
                s1_start(ph, t)
                if after is not None:
                    load(after, buf, sem, t).start()

            guard(tri, used(t), piece)
            for n in subs:
                pl.when(t == kinds + 1 + n)(lambda n=n: gather(ph, 0, n, tri, True))
                pl.when(t == kinds + 1 + n)(lambda n=n: gather(ph, 0, n, tri, False))

    @pl.loop(0, 2 * kinds)
    def _(t):
        load(panel.at[0], pbuf, psem, t).wait()
        part[0, t] = product(pbuf, w0, t)
        load(panel.at[1], pbuf, psem, t).start()

    @pl.when(hub)
    def _():
        for b in range(2):
            side(b).wait()
        pl.loop(0, 2 * kinds)(lambda t: less_side(part.at[0, t], 0, t))

    pl.semaphore_wait(barrier, greeted)
    for k in range(2):
        for n in subs:
            for kind in range(3):
                s1(0, k * kinds + kind, n).start()
    load_all(inv.at[0], buf0, sem0, True)

    @pl.loop(0, 2 * kinds)
    def _(t):
        load(panel.at[1], pbuf, psem, t).wait()
        part1[t] = product(pbuf, w0, t)
        less_side(part1.at[t], 1, t)

    load_all(coup, buf1, sem1, False)
    for n in subs:
        for own in (True, False):
            gather(0, 0, n, False, own)
    reduce(0, False, -1)
    spread(0)
    multiply(1, inv.at[0], buf0, sem0, wv, True, after=inv.at[1])
    reduce(1, True, 1, 0)
    relay_all()
    spread(1)
    multiply(2, coup, buf1, sem1, wv, False, more=True)
    reduce(2, False, -1, between=deliver_all)
    spread(2)
    multiply(3, inv.at[1], buf0, sem0, wv, True)
    reduce(3, True, 1, 1, between=lambda: hand_over(0, 1))
    for ph in range(4):
        drain(ph, ph % 2 == 1)
    for ph in range(3):
        spread_end(ph)
    sent_end(0, 1)
    hand_over(1, 3)
    hand_over_end(0, 1)
    sent_end(1, 3)
    hand_over_end(1, 3)


def paired_call(panel, prior, side, coupling, inverses):
    rows, width = coupling.shape
    r = prior.shape[1]
    pr = rows // 8
    dma = pltpu.SemaphoreType.DMA
    hbm = pl.BlockSpec(memory_space=pl.ANY)
    return pl.pallas_call(
        paired,
        out_shape=jax.ShapeDtypeStruct(side.shape, F32),
        in_specs=[hbm, hbm, hbm, hbm, hbm],
        out_specs=hbm,
        scratch_shapes=[
            pltpu.VMEM((4, 8, r, pr), F32),
            pltpu.VMEM((8, r, pr), F32),
            pltpu.VMEM((4, 6, r, pr), F32),
            pltpu.VMEM((4, 4, r, pr), F32),
            pltpu.VMEM((4, 4, r, pr), F32),
            pltpu.VMEM((2 * r, width), BF16),
            pltpu.VMEM((2 * r, prior.shape[0]), BF16),
            pltpu.VMEM(panel.shape[1:], F32),
            pltpu.VMEM((rows, width), F32),
            pltpu.VMEM((rows, width), F32),
            pltpu.VMEM((2, r, 4 * pr), F32),
            pltpu.VMEM((r, prior.shape[0]), F32),
            pltpu.VMEM((4, r, pr), F32),
            dma((8,)), dma((8,)), dma((8,)), dma((3,)),
            dma((4, 6, SUBS)), dma((4, 6, SUBS)),
            dma((4, 2, 2, SUBS)), dma((4, 4, SUBS)),
            dma((3, 3, SUBS)), dma((3, 4, SUBS)),
            dma((2, 4, SUBS)), dma((2, 4, SUBS)),
            dma((2, 4, SUBS)), dma((2, 4, SUBS)),
            dma((4, SUBS)), dma((4, SUBS)),
        ],
        compiler_params=pltpu.CompilerParams(collective_id=0, has_side_effects=True, vmem_limit_bytes=67043328),
    )(panel, prior.T, side, coupling, inverses)


def shards(nc, nr, panel, prior, right_side, coupling, inverses):
    q = nc // nr
    rows, width = coupling.shape
    r = prior.shape[1]
    pr = rows // nc
    dense = pr % 128 == 0
    lanes = 2 * r
    dma = pltpu.SemaphoreType.DMA
    hbm = pl.BlockSpec(memory_space=pl.ANY)
    vmem = pl.BlockSpec(memory_space=pltpu.VMEM)
    side = right_side.transpose(0, 2, 1)
    if nc == 8 and nr == 4 and dense:
        return paired_call(panel, prior, side, coupling, inverses).transpose(0, 2, 1)
    if not dense:
        side = side.reshape(2, r, nc, pr).transpose(0, 2, 1, 3)
    solved = pl.pallas_call(
        functools.partial(kernel, q, nr),
        out_shape=jax.ShapeDtypeStruct(side.shape, F32),
        in_specs=[hbm, vmem, hbm, hbm, hbm],
        out_specs=vmem,
        scratch_shapes=[
            pltpu.VMEM((q, nr, r, pr), F32),
            pltpu.VMEM((q, nr, r, pr), F32),
            pltpu.VMEM((4, q - 1, nr, r, pr), F32),
            pltpu.VMEM((4, nr - 1, r, pr), F32),
            pltpu.VMEM((4, r, pr), F32),
            pltpu.VMEM((3, nr, r, pr), F32),
            pltpu.VMEM((width, lanes), BF16),
            pltpu.VMEM((prior.shape[0], lanes), BF16),
            pltpu.VMEM(panel.shape[1:], F32),
            pltpu.VMEM((rows, width), F32),
            pltpu.VMEM((rows, width), F32),
            pltpu.VMEM((2, r, pr), F32),
            dma((nc,)), dma((nc,)), dma((nc,)), dma((2,)),
            dma((4, q - 1, nr, SUBS)), dma((4, q - 1, nr, SUBS)),
            dma((4, nr - 1, SUBS)), dma((4, nr - 1, SUBS)),
            dma((3, nr // 2, SUBS)), dma((3, nr, SUBS)), dma((3, nr, SUBS)),
            dma((2, nr - 1, SUBS)), dma((2, nr - 1, SUBS)),
            dma((2, q - 1, nr, SUBS)), dma((2, q - 1, nr, SUBS)),
        ],
        compiler_params=pltpu.CompilerParams(collective_id=0, has_side_effects=True, vmem_limit_bytes=67043328),
    )(panel, prior.T, side, coupling, inverses)
    if not dense:
        solved = solved.transpose(0, 2, 1, 3).reshape(2, r, rows)
    return solved.transpose(0, 2, 1)


def solution(mesh):
    in_specs = (
        P(None, "row", "col"),
        P("col", None),
        P(None, "row", None),
        P("row", "col"),
        P(None, "row", "col"),
    )
    out_specs = P(None, "row", None)
    body = functools.partial(shards, mesh.shape["col"], mesh.shape["row"])
    return jax.shard_map(body, mesh=mesh, in_specs=in_specs, out_specs=out_specs, check_vma=False)
```
